512 devices in a mesh: dp: 4 (over y), cam: 32 (over x, z_lo), slab: 4 (over z_hi, core).
Axes of the slice: x: 4, y: 4, z: 16 (z_hi: 2, z_lo: 8; z = z_hi * 8 + z_lo), core: 2. Of those that a mesh axis runs over, the one named last changes fastest.
Arguments:
- image: bfloat16 [128, 16, 256, 128], P(('dp', 'cam'), 'slab'), parts along dimension 0, may hold values from -6 to 6
- w_first: bfloat16 [3, 3, 128, 128], replicated, may hold values from -0.1875 to 0.1875
- w_second: bfloat16 [3, 3, 128, 128], replicated, may hold values from -0.1875 to 0.1875
- w_reduce: bfloat16 [128, 32], replicated, may hold values from -0.5 to 0.5
- cam_weight: float32 [32], P('cam'), may hold values from 0.3 to 3
- sample_pixel: int32 [512, 128, 32], P(('dp', 'cam', 'slab')), parts along dimension 0, may hold values from 0 to 1022, as said below
- sample_frac: float32 [512, 2, 128, 32], P(('dp', 'cam', 'slab')), parts along dimension 0, may hold values from 0 to 1
- voxel_slot: int32 [512, 128, 32], P(('dp', 'cam', 'slab')), parts along dimension 0, may hold values from 0 to 1024, as said below
- wv_first: bfloat16 [27, 32, 32], replicated, may hold values from -0.21875 to 0.21875
- wv_second: bfloat16 [27, 32, 32], replicated, may hold values from -0.21875 to 0.21875
Outputs:
- volume_out: bfloat16 [32, 256, 2048], P(None, ('dp', 'cam'), 'slab'), parts along dimension 1
The draws below stay inside these ranges and needn't reach their ends.
There are 4 independent parts, one for each index of `dp`. The reference program is written for one: setup_inputs(seed, part) draws one part's arguments, and reference() takes and returns one part's arrays. A program takes and returns all parts, laid end to end along the dimension named above; an argument that names none is the same for every part. Nothing has to cross between parts.
Inputs may be any that keep to these rules, and one draw needn't show every extreme that they name: `sample_pixel`: row * 256 + column of a pixel within the source's 4 rows; the column is at most 254. `voxel_slot`: 1024 marks an empty slot; at most 32 filled slots from one source to one owner, and in every draw some owner receives 32 filled slots from every source.
All inputs are finite; a program needn't handle non-finite values.
Results may differ from the reference program's by a relative error of at most 0.0075.
Values may be sent and summed in bfloat16 or wider, within the bound.
No kernel may reach another device: no remote copies, remote signals or barrier semaphores. Data moves between devices by JAX's collectives and lax.ppermute only.
A program may use at most 64 MiB of HBM per device.

```python
import math
import jax
import jax.numpy as jnp
from jax import lax

C_IMG = 128
VCH = 32
COLS = 256
ROWS_DEV = 4
CAP = 32
BX = 2
BY = 8
VZ = 64
CAMS = 32
DEVS = 128
ROWS = 16
VOX_DEV = 1024
VX = 64
VY = 32
N_CAM = 32
N_SLAB = 4


def draw_sample_pixel(key, part):
    key_row, key_col = jax.random.split(key)
    row_pick = jax.random.randint(key_row, (DEVS, DEVS, CAP), 0, ROWS_DEV)
    col_pick = jax.random.randint(key_col, (DEVS, DEVS, CAP), 0, COLS - 1)
    return (row_pick * COLS + col_pick).astype(jnp.int32)


def draw_voxel_slot(key, part):
    key_load, key_hot, key_count, key_voxel = jax.random.split(key, 4)
    owner_load = jax.random.randint(key_load, (DEVS, 1), 2, 5)
    hot_owner = jax.random.randint(key_hot, (), 0, DEVS)
    raw_count = jax.random.randint(key_count, (DEVS, DEVS), 0, CAP + 1)
    filled = raw_count * owner_load // 4
    owner_ids = jnp.arange(DEVS, dtype=jnp.int32)[:, None]
    filled = jnp.where(owner_ids == hot_owner, CAP, filled)
    slot_ids = jnp.arange(CAP, dtype=jnp.int32)[None, None, :]
    voxels = jax.random.randint(key_voxel, (DEVS, DEVS, CAP), 0, VOX_DEV)
    return jnp.where(slot_ids < filled[:, :, None], voxels, VOX_DEV).astype(jnp.int32)


def steps_of(own_key, extent, shards, low, top_value):
    def one(position, blocks):
        draws = jax.random.uniform(jax.random.fold_in(jax.random.fold_in(own_key, 6), position), (blocks,), jnp.float32, low / len(shards), top_value / len(shards))
        return jnp.repeat(jnp.exp(draws), extent[position] // blocks).reshape((-1,) + (1,) * (len(extent) - position - 1))

    loudness = one(*shards[0])
    for cut in shards[1:]:
        loudness = loudness * one(*cut)
    return loudness


def noise(rng, extent, spread, most, cuts=(), kind=jnp.bfloat16):
    gain = steps_of(rng, extent, cuts, -0.22, 0.18) if cuts else 1.0
    values = jax.random.normal(rng, extent, jnp.float32) * spread * gain
    return jnp.minimum(jnp.maximum(values, -most), most).astype(kind)


def setup_inputs(seed: int = 0, part: int = 0) -> dict:
    key_list = jax.random.split(jax.random.key(seed), 11)
    own_keys = jax.random.split(jax.random.fold_in(key_list[10], part), 11)
    return {
        "image": noise(own_keys[0], (CAMS, ROWS, COLS, C_IMG), 1.0, 6.0, ((0, 32), (1, 4))),
        "w_first": noise(key_list[1], (3, 3, C_IMG, C_IMG), (9 * C_IMG) ** -0.5, 0.1875),
        "w_second": noise(key_list[2], (3, 3, C_IMG, C_IMG), (9 * C_IMG) ** -0.5, 0.1875),
        "w_reduce": noise(key_list[3], (C_IMG, VCH), C_IMG ** -0.5, 0.5),
        "cam_weight": jnp.clip(jnp.exp(math.log(3.0) - 2.3025851 * jax.random.uniform(key_list[4], (CAMS,), jnp.float32) ** steps_of(key_list[4], (CAMS,), ((0, 32),), -0.2, 0.2)), 0.3, 3.0),
        "sample_pixel": draw_sample_pixel(jax.random.fold_in(jax.random.fold_in(key_list[10], part), 71), part),
        "sample_frac": jnp.clip(1.0 * jax.random.uniform(own_keys[6], (DEVS, 2, DEVS, CAP), jnp.float32) ** steps_of(own_keys[6], (DEVS, 2, DEVS, CAP), ((0, 128),), -0.2, 0.2), 0.0, 1.0),
        "voxel_slot": draw_voxel_slot(jax.random.fold_in(jax.random.fold_in(key_list[10], part), 71), part),
        "wv_first": noise(key_list[8], (27, VCH, VCH), (27 * VCH) ** -0.5, 0.21875),
        "wv_second": noise(key_list[9], (27, VCH, VCH), (27 * VCH) ** -0.5, 0.21875),
    }


def image_conv(padded, weight, row_count, col_count):
    running = jnp.zeros((row_count * col_count, weight.shape[3]), jnp.float32)
    for row_off in range(3):
        for col_off in range(3):
            window = padded[row_off:row_off + row_count, col_off:col_off + col_count, :]
            window = window.reshape(row_count * col_count, weight.shape[2])
            running = running + jnp.dot(window, weight[row_off, col_off], preferred_element_type=jnp.float32)
    return running


def bilinear(table, pixel, frac_row, frac_col, col_count, scale):
    top_left = jnp.take(table, pixel, axis=1).astype(jnp.float32)
    top_right = jnp.take(table, pixel + 1, axis=1).astype(jnp.float32)
    low_left = jnp.take(table, pixel + col_count, axis=1).astype(jnp.float32)
    low_right = jnp.take(table, pixel + col_count + 1, axis=1).astype(jnp.float32)
    upper = (1.0 - frac_col) * top_left + frac_col * top_right
    lower = (1.0 - frac_col) * low_left + frac_col * low_right
    return ((1.0 - frac_row) * upper + frac_row * lower) * scale


def volume_conv(volume, weight):
    padded = jnp.pad(volume, ((0, 0), (1, 1), (1, 1), (1, 1)))
    running = jnp.zeros((VCH, VX * VY * VZ), jnp.float32)
    for plane_off in range(3):
        for row_off in range(3):
            for depth_off in range(3):
                window = padded[:, plane_off:plane_off + VX, row_off:row_off + VY, depth_off:depth_off + VZ]
                running = running + jnp.dot(weight[(plane_off * 3 + row_off) * 3 + depth_off],
                                            window.reshape(VCH, VX * VY * VZ),
                                            preferred_element_type=jnp.float32)
    return running


def reference(image, w_first, w_second, w_reduce, cam_weight, sample_pixel, sample_frac, voxel_slot, wv_first, wv_second):
    def camera_features(frame_view):
        padded = jnp.pad(frame_view, ((1, 1), (1, 1), (0, 0)))
        hidden = jax.nn.relu(image_conv(padded, w_first, ROWS, COLS)).astype(jnp.bfloat16)
        hidden = hidden.reshape(ROWS, COLS, C_IMG)
        padded = jnp.pad(hidden, ((1, 1), (1, 1), (0, 0)))
        second = jax.nn.relu(image_conv(padded, w_second, ROWS, COLS)).astype(jnp.bfloat16)
        reduced = lax.dot_general(w_reduce, second, (((0,), (1,)), ((), ())),
                                  preferred_element_type=jnp.float32).astype(jnp.bfloat16)
        return jnp.concatenate([reduced, jnp.zeros((VCH, COLS), jnp.bfloat16)], axis=1)

    features = lax.map(camera_features, image)

    def one_source(source):
        camera = source // N_SLAB
        slab_pos = source % N_SLAB
        table = features[camera]
        pixel = sample_pixel[source].reshape(-1) + slab_pos * (ROWS_DEV * COLS)
        fracs = sample_frac[source]
        values = bilinear(table, pixel, fracs[0].reshape(-1), fracs[1].reshape(-1), COLS, cam_weight[camera])
        return values.astype(jnp.bfloat16).reshape(VCH, DEVS, CAP)

    samples = lax.map(one_source, jnp.arange(DEVS, dtype=jnp.int32))

    def one_owner(owner):
        gathered = samples[:, :, owner, :]
        gathered = jnp.transpose(gathered, (0, 2, 1)).reshape(DEVS * CAP, VCH).astype(jnp.float32)
        summed = jax.ops.segment_sum(gathered, voxel_slot[owner].reshape(-1), num_segments=VOX_DEV + 1)
        return summed[:VOX_DEV].T.astype(jnp.bfloat16)

    owned = lax.map(one_owner, jnp.arange(DEVS, dtype=jnp.int32))
    volume = owned.reshape(N_CAM, N_SLAB, VCH, BX, BY, VZ)
    volume = jnp.transpose(volume, (2, 0, 3, 1, 4, 5)).reshape(VCH, VX, VY, VZ)
    vfirst = jax.nn.relu(volume_conv(volume, wv_first)).astype(jnp.bfloat16).reshape(VCH, VX, VY, VZ)
    result = volume_conv(vfirst, wv_second) + volume.reshape(VCH, VX * VY * VZ).astype(jnp.float32)
    return result.astype(jnp.bfloat16).reshape(VCH, VX, VY * VZ)
```

```python
import jax
import jax.numpy as jnp
from jax import lax
from jax.experimental import pallas as pl
from jax.experimental.pallas import tpu as pltpu
from jax.sharding import PartitionSpec as P

AXES = ("cam", "slab")
F32 = jnp.float32
BF16 = jnp.bfloat16


def dot(a, b):
    return jnp.dot(a, b, preferred_element_type=F32)


def dot_nt(a, b):
    return lax.dot_general(a, b, (((1,), (1,)), ((), ())), preferred_element_type=F32)


def whole(memory_space):
    return pl.BlockSpec(memory_space=memory_space)


def put_columns(dst, row, x):
    cols = x.shape[0]
    pos = lax.broadcasted_iota(jnp.int32, x.shape, 0)
    left = jnp.where(pos == 0, 0.0, pltpu.roll(x, 1, 0))
    right = jnp.where(pos == cols - 1, 0.0, pltpu.roll(x, cols - 1, 0))
    dst[row, :, 0:128] = left.astype(BF16)
    dst[row, :, 128:256] = x.astype(BF16)
    dst[row, :, 256:384] = right.astype(BF16)


def features_kernel(
    pos_ref,
    scale_ref,
    img_ref,
    far_ref,
    core_ref,
    w1_ref,
    w2_ref,
    wr_ref,
    pix_ref,
    frac_ref,
    out_ref,
    x1,
    x2,
    acc,
    packed,
):
    slab = pos_ref[0]
    even = (1 - slab % 2).astype(F32)
    odd = 1.0 - even
    not_first = jnp.where(slab == 0, 0.0, 1.0)
    not_last = jnp.where(slab == 3, 0.0, 1.0)
    for i in range(2):
        row = even * far_ref[1 + i].astype(F32) + odd * core_ref[1 + i].astype(F32)
        put_columns(x1, i, row)
    for i in range(4):
        put_columns(x1, 2 + i, img_ref[i].astype(F32))
    for i in range(3):
        row = even * core_ref[i].astype(F32) + odd * far_ref[i].astype(F32)
        put_columns(x1, 6 + i, row)
    acc[...] = dot(x1[0:7].reshape(1792, 384), w1_ref[0])
    acc[...] += dot(x1[1:8].reshape(1792, 384), w1_ref[1])
    acc[...] += dot(x1[2:9].reshape(1792, 384), w1_ref[2])
    for i in range(7):
        h = jnp.maximum(acc[i * 256 : (i + 1) * 256], 0.0)
        if i == 0:
            h = h * not_first
        if i >= 5:
            h = h * not_last
        put_columns(x2, i, h)
    acc[0:1280] = dot(x2[0:5].reshape(1280, 384), w2_ref[0])
    acc[0:1280] += dot(x2[1:6].reshape(1280, 384), w2_ref[1])
    acc[0:1280] += dot(x2[2:7].reshape(1280, 384), w2_ref[2])
    table = []
    for i in range(5):
        h = jnp.maximum(acc[i * 256 : (i + 1) * 256], 0.0)
        if i == 4:
            h = h * not_last
        table.append(dot_nt(wr_ref[...], h.astype(BF16)))
    table = jnp.concatenate(table, axis=0).astype(BF16)
    scale = scale_ref[0]
    col_iota = lax.broadcasted_iota(jnp.int32, (256, 512), 0)

    def lanes(x):
        return jnp.concatenate([x[i : i + 1] for i in range(4)], axis=1)

    for k in range(8):
        pix = lanes(pix_ref[4 * k : 4 * k + 4])
        fr = lanes(frac_ref[0, 4 * k : 4 * k + 4])
        fc = lanes(frac_ref[1, 4 * k : 4 * k + 4])
        col = pix & 255
        row = pix >> 8
        weights = jnp.where(
            col_iota == col, 1.0 - fc, jnp.where(col_iota == col + 1, fc, 0.0)
        ).astype(BF16)
        got = dot(table, weights)
        total = None
        for r in range(5):
            blend = jnp.where(row == r, 1.0 - fr, jnp.where(row == r - 1, fr, 0.0)) * scale
            part = got[32 * r : 32 * r + 32] * blend
            total = part if total is None else total + part
        block = jnp.concatenate([total[:, 128 * i : 128 * i + 128] for i in range(4)], axis=0)
        packed[pl.ds(k, 128, stride=8), :] = block.T
    out_ref[...] = packed[...].astype(BF16)


def features(slab, scale, img, far, core, w1, w2, wr, pix, frac):
    return pl.pallas_call(
        features_kernel,
        out_shape=jax.ShapeDtypeStruct((1024, 128), BF16),
        in_specs=[whole(pltpu.SMEM)] * 2 + [whole(pltpu.VMEM)] * 8,
        out_specs=whole(pltpu.VMEM),
        scratch_shapes=[
            pltpu.VMEM((9, 256, 384), BF16),
            pltpu.VMEM((7, 256, 384), BF16),
            pltpu.VMEM((1792, 128), F32),
            pltpu.VMEM((1024, 128), F32),
        ],
        compiler_params=pltpu.CompilerParams(vmem_limit_bytes=40 * 2**20),
        name="features",
    )(slab, scale, img, far, core, w1, w2, wr, pix, frac)


def scatter_kernel(val_ref, by_lane_ref, by_row_ref, out_ref):
    val = val_ref[...]
    lo_iota = lax.broadcasted_iota(jnp.int32, (256, 1024), 0)
    hi_iota = lax.broadcasted_iota(jnp.int32, (1024, 128), 1) // 32
    sel_row = lax.broadcasted_iota(jnp.int32, (128, 128), 0)
    sel_col = lax.broadcasted_iota(jnp.int32, (128, 128), 1) % 32
    total = jnp.zeros((256, 128), F32)
    for s in range(4):
        one_hot = jnp.where(lo_iota == (by_lane_ref[s : s + 1] >> 2), 1.0, 0.0).astype(BF16)
        select = jnp.where(sel_row == sel_col + 32 * s, 1.0, 0.0).astype(BF16)
        spread = dot(val, select)
        hi = by_row_ref[:, s : s + 1] & 3
        spread = jnp.where(hi_iota == hi, spread, 0.0).astype(BF16)
        total = total + dot(one_hot, spread)
    out_ref[...] = total.reshape(2, 128, 128).astype(BF16)


def scatter(val, by_lane, by_row):
    return pl.pallas_call(
        scatter_kernel,
        out_shape=jax.ShapeDtypeStruct((2, 128, 128), BF16),
        in_specs=[whole(pltpu.VMEM)] * 3,
        out_specs=whole(pltpu.VMEM),
        compiler_params=pltpu.CompilerParams(vmem_limit_bytes=40 * 2**20),
        name="scatter",
    )(val, by_lane, by_row)


def put_depth(dst, plane, x):
    step = lax.broadcasted_iota(jnp.int32, x.shape, 0) % 16
    lane = lax.broadcasted_iota(jnp.int32, x.shape, 1)
    rows = x.shape[0]
    before = jnp.where(step == 0, 0.0, pltpu.roll(x, 1, 0))
    after = jnp.where(step == 15, 0.0, pltpu.roll(x, rows - 1, 0))
    side = pltpu.roll(jnp.where(lane >= 96, before, after), 32, 1)
    dst[plane, :, 0:128] = x.astype(BF16)
    dst[plane, :, 128:256] = jnp.where(lane < 64, side, 0.0).astype(BF16)


def volume_kernel(pos_ref, own_ref, near_ref, next_ref, w1_ref, w2_ref, out_ref, x1, x2, acc):
    p = pos_ref[0]
    q = pos_ref[1]
    even = (1 - p % 2).astype(F32)
    odd = 1.0 - even
    for i in range(2):
        near = near_ref[i].astype(F32)
        nxt = next_ref[i].astype(F32)
        put_depth(x1, i, even * nxt + odd * near)
        put_depth(x1, 2 + i, own_ref[i].astype(F32))
        put_depth(x1, 4 + i, even * near + odd * nxt)
    for t in range(9):
        dx, dy = divmod(t, 3)
        part = dot_nt(x1[dx : dx + 4, dy * 16 : dy * 16 + 160, :].reshape(640, 256), w1_ref[t])
        if t == 0:
            acc[...] = part
        else:
            acc[...] += part
    y = lax.broadcasted_iota(jnp.int32, (160, 128), 0) // 16
    first_y = jnp.where(q == 0, 1, 0)
    last_y = jnp.where(q == 3, 8, 9)
    inside = (y >= first_y) & (y <= last_y)
    for i in range(4):
        h = jnp.where(inside, jnp.maximum(acc[i * 160 : (i + 1) * 160], 0.0), 0.0)
        if i == 0:
            h = h * jnp.where(p == 0, 0.0, 1.0)
        if i == 3:
            h = h * jnp.where(p == 31, 0.0, 1.0)
        put_depth(x2, i, h)
    for t in range(9):
        dx, dy = divmod(t, 3)
        part = dot_nt(x2[dx : dx + 2, dy * 16 : dy * 16 + 128, :].reshape(256, 256), w2_ref[t])
        if t == 0:
            acc[0:256] = part
        else:
            acc[0:256] += part
    place_row = lax.broadcasted_iota(jnp.int32, (128, 512), 0) * 4
    place_col = lax.broadcasted_iota(jnp.int32, (128, 512), 1)
    for i in range(2):
        res = acc[i * 128 : (i + 1) * 128] + own_ref[i, 32:160].astype(F32)
        res = res.T.astype(BF16)
        total = jnp.zeros((32, 512), F32)
        for z in range(4):
            place = jnp.where(place_col == place_row + z, 1.0, 0.0).astype(BF16)
            total = total + dot(res[32 * z : 32 * z + 32], place)
        out_ref[:, 512 * i : 512 * i + 512] = total.astype(BF16)


def volume_convs(pos, own, near, nxt, w1, w2):
    return pl.pallas_call(
        volume_kernel,
        out_shape=jax.ShapeDtypeStruct((32, 1024), BF16),
        in_specs=[whole(pltpu.SMEM)] + [whole(pltpu.VMEM)] * 5,
        out_specs=whole(pltpu.VMEM),
        scratch_shapes=[
            pltpu.VMEM((6, 192, 256), BF16),
            pltpu.VMEM((4, 160, 256), BF16),
            pltpu.VMEM((640, 128), F32),
        ],
        compiler_params=pltpu.CompilerParams(vmem_limit_bytes=40 * 2**20),
        name="volume",
    )(pos, own, near, nxt, w1, w2)


def banded(weight):
    taps = weight.reshape(9, 3, 32, 32)
    zero = jnp.zeros((9, 32, 32), weight.dtype)
    rows = []
    for z in range(4):
        blocks = [zero] * 8
        for dz in range(3):
            at = z + dz - 1
            blocks[4 if at < 0 else 5 if at > 3 else at] = taps[:, dz]
        rows.append(jnp.concatenate(blocks, axis=2))
    return jnp.concatenate(rows, axis=1)


def swap(x, partner, cams, slabs):
    pairs = []
    for p in range(cams):
        for s in range(slabs):
            to = partner(p, s)
            if 0 <= to[0] < cams and 0 <= to[1] < slabs:
                pairs.append((p * slabs + s, to[0] * slabs + to[1]))
    return lax.ppermute(x, AXES, pairs)


def core_partner(p, s):
    return p, s ^ 1


def far_partner(p, s):
    return p, (s + 1 if s % 2 else s - 1)


def near_partner(p, s):
    return p ^ 1, s


def next_partner(p, s):
    return (p + 1 if p % 2 else p - 1), s


def local(
    image,
    w_first,
    w_second,
    w_reduce,
    cam_weight,
    sample_pixel,
    sample_frac,
    voxel_slot,
    wv_first,
    wv_second,
):
    cams = lax.axis_size("cam")
    slabs = lax.axis_size("slab")
    p = lax.axis_index("cam")
    s = lax.axis_index("slab")
    even = s % 2 == 0
    img = image[0]
    top, bottom = img[0:3], img[1:4]
    far = swap(jnp.where(even, top, bottom), far_partner, cams, slabs)
    core = swap(jnp.where(even, bottom, top), core_partner, cams, slabs)

    pix = sample_pixel[0].T
    frac = jnp.transpose(sample_frac[0], (0, 2, 1))
    w1 = w_first.reshape(3, 384, 128)
    w2 = w_second.reshape(3, 384, 128)
    by_row = voxel_slot[0].reshape(1024, 4)
    by_lane = by_row.T
    band1 = banded(wv_first)
    band2 = banded(wv_second)
    slab_pos = s.astype(jnp.int32).reshape(1)
    pos = jnp.stack([p, s]).astype(jnp.int32)

    sent = features(slab_pos, cam_weight, img, far, core, w1, w2, w_reduce.T, pix, frac)
    got = lax.all_to_all(sent.reshape(128, 8, 128), AXES, 0, 0, tiled=True).reshape(1024, 128)
    volume = scatter(got, by_lane, by_row)

    top, bottom = volume[:, 0:32], volume[:, 96:128]
    far = swap(jnp.where(even, top, bottom), far_partner, cams, slabs)
    core = swap(jnp.where(even, bottom, top), core_partner, cams, slabs)
    above = jnp.where(even, far, core)
    below = jnp.where(even, core, far)
    own = jnp.concatenate([above, volume, below], axis=1)
    near = swap(own, near_partner, cams, slabs)
    nxt = swap(own, next_partner, cams, slabs)
    out = volume_convs(pos, own, near, nxt, band1, band2)
    return out.reshape(32, 2, 512)


def solution(mesh):
    placed = (
        P(("dp", "cam"), "slab", None, None),
        P(),
        P(),
        P(),
        P("cam"),
        P(("dp", "cam", "slab"), None, None),
        P(("dp", "cam", "slab"), None, None, None),
        P(("dp", "cam", "slab"), None, None),
        P(),
        P(),
    )
    return jax.shard_map(
        local, mesh=mesh, in_specs=placed, out_specs=P(None, ("dp", "cam"), "slab"), check_vma=False
    )
```

```python
import jax
import jax.numpy as jnp
from jax import lax
from jax.experimental import pallas as pl
from jax.experimental.pallas import tpu as pltpu
from jax.sharding import PartitionSpec as P

AXES = ("cam", "slab")
F32 = jnp.float32
BF16 = jnp.bfloat16


def dot(a, b):
    return jnp.dot(a, b, preferred_element_type=F32)


def dot_nt(a, b):
    return lax.dot_general(a, b, (((1,), (1,)), ((), ())), preferred_element_type=F32)


def whole(memory_space):
    return pl.BlockSpec(memory_space=memory_space)


def put_columns(dst, row, x):
    cols = x.shape[0]
    pos = lax.broadcasted_iota(jnp.int32, x.shape, 0)
    left = jnp.where(pos == 0, 0.0, pltpu.roll(x, 1, 0))
    right = jnp.where(pos == cols - 1, 0.0, pltpu.roll(x, cols - 1, 0))
    dst[row, :, 0:128] = left.astype(BF16)
    dst[row, :, 128:256] = x.astype(BF16)
    dst[row, :, 256:384] = right.astype(BF16)


def lanes(x):
    return jnp.concatenate([x[i : i + 1] for i in range(4)], axis=1)


def prepare_kernel(scale_ref, img_ref, w1_ref, pix_ref, frac_ref, acc, weights, blends, x1):
    for i in range(4):
        put_columns(x1, i, img_ref[i].astype(F32))
    own = x1[...].reshape(1024, 384)
    acc[0:512] = jnp.zeros((512, 128), F32)
    acc[1536:1792] = jnp.zeros((256, 128), F32)
    acc[512:1536] = dot(own, w1_ref[0])
    acc[256:1280] += dot(own, w1_ref[1])
    acc[0:1024] += dot(own, w1_ref[2])
    scale = scale_ref[0]
    col_iota = lax.broadcasted_iota(jnp.int32, (256, 512), 0)
    row_iota = lax.broadcasted_iota(jnp.int32, (8, 512), 0)
    for k in range(8):
        pix = lanes(pix_ref[4 * k : 4 * k + 4])
        fr = lanes(frac_ref[0, 4 * k : 4 * k + 4])
        fc = lanes(frac_ref[1, 4 * k : 4 * k + 4])
        col = pix & 255
        row = pix >> 8
        weights[k] = jnp.where(
            col_iota == col, 1.0 - fc, jnp.where(col_iota == col + 1, fc, 0.0)
        ).astype(BF16)
        blends[k] = scale * jnp.where(
            row_iota == row, 1.0 - fr, jnp.where(row_iota == row + 1, fr, 0.0)
        )


def prepare(scale, img, w1, pix, frac):
    return pl.pallas_call(
        prepare_kernel,
        out_shape=(
            jax.ShapeDtypeStruct((1792, 128), F32),
            jax.ShapeDtypeStruct((8, 256, 512), BF16),
            jax.ShapeDtypeStruct((8, 8, 512), F32),
        ),
        in_specs=[whole(pltpu.SMEM)] + [whole(pltpu.VMEM)] * 4,
        out_specs=(whole(pltpu.VMEM),) * 3,
        scratch_shapes=[pltpu.VMEM((4, 256, 384), BF16)],
        compiler_params=pltpu.CompilerParams(vmem_limit_bytes=24 * 2**20),
        cost_estimate=pl.CostEstimate(flops=10**9, bytes_accessed=4 * 10**6, transcendentals=0),
        name="prepare",
    )(scale, img, w1, pix, frac)


def features_kernel(
    pos_ref, far_ref, core_ref, w1_ref, w2_ref, wr_ref, part_ref, weights, blends, out_ref,
    x1, x2, acc, packed,
):
    slab = pos_ref[0]
    even = (1 - slab % 2).astype(F32)
    odd = 1.0 - even
    not_first = jnp.where(slab == 0, 0.0, 1.0)
    not_last = jnp.where(slab == 3, 0.0, 1.0)
    for i in range(2):
        row = even * far_ref[1 + i].astype(F32) + odd * core_ref[1 + i].astype(F32)
        put_columns(x1, i, row)
    for i in range(3):
        row = even * core_ref[i].astype(F32) + odd * far_ref[i].astype(F32)
        put_columns(x1, 2 + i, row)
    head = dot(x1[0:2].reshape(512, 384), w1_ref[0])
    head0 = head[0:256] + dot(x1[1], w1_ref[1])
    tail0 = dot(x1[2:3].reshape(256, 384), w1_ref[0])
    tail1 = dot(x1[2:4].reshape(512, 384), w1_ref[1])
    tail2 = dot(x1[2:5].reshape(768, 384), w1_ref[2])
    for i in range(7):
        h = part_ref[i * 256 : (i + 1) * 256]
        if i == 0:
            h = h + head0
        elif i == 1:
            h = h + head[256:512]
        elif i == 4:
            h = h + tail2[0:256]
        elif i == 5:
            h = h + tail2[256:512] + tail1[0:256]
        elif i == 6:
            h = h + tail2[512:768] + tail1[256:512] + tail0
        h = jnp.maximum(h, 0.0)
        if i == 0:
            h = h * not_first
        if i >= 5:
            h = h * not_last
        put_columns(x2, i, h)
    acc[...] = dot(x2[0:5].reshape(1280, 384), w2_ref[0])
    acc[...] += dot(x2[1:6].reshape(1280, 384), w2_ref[1])
    acc[...] += dot(x2[2:7].reshape(1280, 384), w2_ref[2])
    table = []
    for i in range(5):
        h = jnp.maximum(acc[i * 256 : (i + 1) * 256], 0.0)
        if i == 4:
            h = h * not_last
        table.append(dot_nt(wr_ref[...], h.astype(BF16)))
    table = jnp.concatenate(table, axis=0).astype(BF16)
    for k in range(8):
        got = dot(table, weights[k])
        blend = blends[k]
        total = got[0:32] * blend[0:1]
        for r in range(1, 5):
            total = total + got[32 * r : 32 * r + 32] * blend[r : r + 1]
        block = jnp.concatenate([total[:, 128 * i : 128 * i + 128] for i in range(4)], axis=0)
        packed[pl.ds(k, 128, stride=8), :] = block.T
    out_ref[...] = packed[...].astype(BF16)


def features(slab, far, core, w1, w2, wr, part, weights, blends):
    return pl.pallas_call(
        features_kernel,
        out_shape=jax.ShapeDtypeStruct((1024, 128), BF16),
        in_specs=[whole(pltpu.SMEM)] + [whole(pltpu.VMEM)] * 8,
        out_specs=whole(pltpu.VMEM),
        scratch_shapes=[
            pltpu.VMEM((5, 256, 384), BF16),
            pltpu.VMEM((7, 256, 384), BF16),
            pltpu.VMEM((1280, 128), F32),
            pltpu.VMEM((1024, 128), F32),
        ],
        compiler_params=pltpu.CompilerParams(vmem_limit_bytes=32 * 2**20),
        name="features",
    )(slab, far, core, w1, w2, wr, part, weights, blends)


def scatter_kernel(val_ref, by_lane_ref, by_row_ref, out_ref):
    val = val_ref[...]
    lo_iota = lax.broadcasted_iota(jnp.int32, (256, 1024), 0)
    hi_iota = lax.broadcasted_iota(jnp.int32, (1024, 128), 1) // 32
    sel_row = lax.broadcasted_iota(jnp.int32, (128, 128), 0)
    sel_col = lax.broadcasted_iota(jnp.int32, (128, 128), 1) % 32
    total = jnp.zeros((256, 128), F32)
    for s in range(4):
        one_hot = jnp.where(lo_iota == (by_lane_ref[s : s + 1] >> 2), 1.0, 0.0).astype(BF16)
        select = jnp.where(sel_row == sel_col + 32 * s, 1.0, 0.0).astype(BF16)
        spread = dot(val, select)
        hi = by_row_ref[:, s : s + 1] & 3
        spread = jnp.where(hi_iota == hi, spread, 0.0).astype(BF16)
        total = total + dot(one_hot, spread)
    out_ref[...] = total.reshape(2, 128, 128).astype(BF16)


def scatter(val, by_lane, by_row):
    return pl.pallas_call(
        scatter_kernel,
        out_shape=jax.ShapeDtypeStruct((2, 128, 128), BF16),
        in_specs=[whole(pltpu.VMEM)] * 3,
        out_specs=whole(pltpu.VMEM),
        compiler_params=pltpu.CompilerParams(vmem_limit_bytes=40 * 2**20),
        name="scatter",
    )(val, by_lane, by_row)


def put_depth(dst, plane, x):
    step = lax.broadcasted_iota(jnp.int32, x.shape, 0) % 16
    lane = lax.broadcasted_iota(jnp.int32, x.shape, 1)
    rows = x.shape[0]
    before = jnp.where(step == 0, 0.0, pltpu.roll(x, 1, 0))
    after = jnp.where(step == 15, 0.0, pltpu.roll(x, rows - 1, 0))
    side = pltpu.roll(jnp.where(lane >= 96, before, after), 32, 1)
    dst[plane, :, 0:128] = x.astype(BF16)
    dst[plane, :, 128:256] = jnp.where(lane < 64, side, 0.0).astype(BF16)


def volume_kernel(pos_ref, own_ref, quad_ref, near_ref, core_ref, w1_ref, w2_ref, out_ref, x1, x2, acc):
    p = pos_ref[0]
    q = pos_ref[1]
    me = pos_ref[2]
    even_p = p % 2 == 0
    even_q = q % 2 == 0
    has_next = jnp.where((p == 0) | (p == 31), 0.0, 1.0)
    has_far = jnp.where((q == 0) | (q == 3), 0.0, 1.0)
    next_at = jnp.where(even_p, 0, 4)
    near_at = 4 - next_at
    far_from = pl.multiple_of(jnp.where(even_q, 96, 0), 32)
    for i in range(2):
        nxt = quad_ref[me ^ 1, i].astype(F32) * has_next
        far = quad_ref[me ^ 2, i, pl.ds(far_from, 32)].astype(F32) * has_far
        diag = quad_ref[me ^ 3, i, pl.ds(far_from, 32)].astype(F32) * (has_far * has_next)
        groups = (
            (2 + i, own_ref[i].astype(F32), far, core_ref[i].astype(F32)),
            (next_at + i, nxt, diag, core_ref[2 + i].astype(F32) * has_next),
            (
                near_at + i,
                near_ref[i, 32:160].astype(F32),
                near_ref[i, 0:32].astype(F32),
                core_ref[4 + i].astype(F32),
            ),
        )
        for plane, mid, far_rows, core_rows in groups:
            above = jnp.where(even_q, far_rows, core_rows)
            below = jnp.where(even_q, core_rows, far_rows)
            put_depth(x1, plane, jnp.concatenate([above, mid, below], axis=0))
    for t in range(9):
        dx, dy = divmod(t, 3)
        part = dot_nt(x1[dx : dx + 4, dy * 16 : dy * 16 + 160, :].reshape(640, 256), w1_ref[t])
        if t == 0:
            acc[...] = part
        else:
            acc[...] += part
    y = lax.broadcasted_iota(jnp.int32, (160, 128), 0) // 16
    first_y = jnp.where(q == 0, 1, 0)
    last_y = jnp.where(q == 3, 8, 9)
    inside = (y >= first_y) & (y <= last_y)
    for i in range(4):
        h = jnp.where(inside, jnp.maximum(acc[i * 160 : (i + 1) * 160], 0.0), 0.0)
        if i == 0:
            h = h * jnp.where(p == 0, 0.0, 1.0)
        if i == 3:
            h = h * jnp.where(p == 31, 0.0, 1.0)
        put_depth(x2, i, h)
    for t in range(9):
        dx, dy = divmod(t, 3)
        part = dot_nt(x2[dx : dx + 2, dy * 16 : dy * 16 + 128, :].reshape(256, 256), w2_ref[t])
        if t == 0:
            acc[0:256] = part
        else:
            acc[0:256] += part
    place_row = lax.broadcasted_iota(jnp.int32, (128, 512), 0) * 4
    place_col = lax.broadcasted_iota(jnp.int32, (128, 512), 1)
    planes = []
    for i in range(2):
        res = acc[i * 128 : (i + 1) * 128] + own_ref[i].astype(F32)
        res = res.T.astype(BF16)
        total = jnp.zeros((32, 512), F32)
        for z in range(4):
            place = jnp.where(place_col == place_row + z, 1.0, 0.0).astype(BF16)
            total = total + dot(res[32 * z : 32 * z + 32], place)
        planes.append(total)
    out_ref[...] = jnp.stack(planes, axis=1).astype(BF16)


def volume_convs(pos, own, quad, near, core, w1, w2):
    return pl.pallas_call(
        volume_kernel,
        out_shape=jax.ShapeDtypeStruct((32, 2, 512), BF16),
        in_specs=[whole(pltpu.SMEM)] + [whole(pltpu.VMEM)] * 6,
        out_specs=whole(pltpu.VMEM),
        scratch_shapes=[
            pltpu.VMEM((6, 192, 256), BF16),
            pltpu.VMEM((4, 160, 256), BF16),
            pltpu.VMEM((640, 128), F32),
        ],
        compiler_params=pltpu.CompilerParams(vmem_limit_bytes=32 * 2**20),
        name="volume",
    )(pos, own, quad, near, core, w1, w2)


def banded(weight):
    taps = weight.reshape(9, 3, 32, 32)
    zero = jnp.zeros((9, 32, 32), weight.dtype)
    rows = []
    for z in range(4):
        blocks = [zero] * 8
        for dz in range(3):
            at = z + dz - 1
            blocks[4 if at < 0 else 5 if at > 3 else at] = taps[:, dz]
        rows.append(jnp.concatenate(blocks, axis=2))
    return jnp.concatenate(rows, axis=1)


def swap(x, partner, cams, slabs):
    pairs = []
    for p in range(cams):
        for s in range(slabs):
            to = partner(p, s)
            if 0 <= to[0] < cams and 0 <= to[1] < slabs:
                pairs.append((p * slabs + s, to[0] * slabs + to[1]))
    return lax.ppermute(x, AXES, pairs)


def core_partner(p, s):
    return p, s ^ 1


def far_partner(p, s):
    return p, (s + 1 if s % 2 else s - 1)


def near_partner(p, s):
    return p ^ 1, s


def quads(cams, slabs):
    groups = []
    for odd in range(1, cams, 2):
        for low in range(slabs // 2):
            groups.append(
                [
                    c % cams * slabs + t
                    for t in (low, slabs - 1 - low)
                    for c in (odd, odd + 1)
                ]
            )
    return groups


def local(
    image,
    w_first,
    w_second,
    w_reduce,
    cam_weight,
    sample_pixel,
    sample_frac,
    voxel_slot,
    wv_first,
    wv_second,
):
    cams = lax.axis_size("cam")
    slabs = lax.axis_size("slab")
    p = lax.axis_index("cam")
    s = lax.axis_index("slab")
    even = s % 2 == 0
    img = image[0]
    top, bottom = img[0:3], img[1:4]
    far = swap(jnp.where(even, top, bottom), far_partner, cams, slabs)
    core = swap(jnp.where(even, bottom, top), core_partner, cams, slabs)

    pix = sample_pixel[0].T
    frac = jnp.transpose(sample_frac[0], (0, 2, 1))
    w1 = w_first.reshape(3, 384, 128)
    w2 = w_second.reshape(3, 384, 128)
    by_row = voxel_slot[0].reshape(1024, 4)
    by_lane = by_row.T
    band1 = banded(wv_first)
    band2 = banded(wv_second)
    slab_pos = s.astype(jnp.int32).reshape(1)

    part, weights, blends = prepare(cam_weight, img, w1, pix, frac)
    sent = features(slab_pos, far, core, w1, w2, w_reduce.T, part, weights, blends)
    got = lax.all_to_all(sent.reshape(128, 8, 128), AXES, 0, 0, tiled=True).reshape(1024, 128)
    own = scatter(got, by_lane, by_row)

    quad = lax.all_gather(own, AXES, axis_index_groups=quads(cams, slabs))
    me = (1 - p % 2) + 2 * (s // 2)
    pos = jnp.stack([p, s, me]).astype(jnp.int32)
    has_far = (s == 1) | (s == 2)
    far = lax.dynamic_index_in_dim(quad, me ^ 2, 0, keepdims=False)
    far = jnp.where(even, far[:, 96:128], far[:, 0:32])
    far = jnp.where(has_far, far, jnp.zeros_like(far))
    near = swap(jnp.concatenate([far, own], axis=1), near_partner, cams, slabs)
    nxt = lax.dynamic_index_in_dim(quad, me ^ 1, 0, keepdims=False)
    core = jnp.where(
        even,
        jnp.concatenate([own[:, 96:128], nxt[:, 96:128], near[:, 128:160]], axis=0),
        jnp.concatenate([own[:, 0:32], nxt[:, 0:32], near[:, 32:64]], axis=0),
    )
    core = swap(core, core_partner, cams, slabs)
    return volume_convs(pos, own, quad, near, core, band1, band2)


def solution(mesh):
    placed = (
        P(("dp", "cam"), "slab", None, None),
        P(),
        P(),
        P(),
        P("cam"),
        P(("dp", "cam", "slab"), None, None),
        P(("dp", "cam", "slab"), None, None, None),
        P(("dp", "cam", "slab"), None, None),
        P(),
        P(),
    )
    return jax.shard_map(
        local, mesh=mesh, in_specs=placed, out_specs=P(None, ("dp", "cam"), "slab"), check_vma=False
    )
```

```python
import jax
import jax.numpy as jnp
from jax import lax
from jax.experimental import pallas as pl
from jax.experimental.pallas import tpu as pltpu
from jax.sharding import PartitionSpec as P

AXES = ("cam", "slab")
F32 = jnp.float32
BF16 = jnp.bfloat16


def dot(a, b):
    return jnp.dot(a, b, preferred_element_type=F32)


def dot_nt(a, b):
    return lax.dot_general(a, b, (((1,), (1,)), ((), ())), preferred_element_type=F32)


def whole(memory_space):
    return pl.BlockSpec(memory_space=memory_space)


def put_columns(dst, row, x):
    cols = x.shape[0]
    pos = lax.broadcasted_iota(jnp.int32, x.shape, 0)
    left = jnp.where(pos == 0, 0.0, pltpu.roll(x, 1, 0))
    right = jnp.where(pos == cols - 1, 0.0, pltpu.roll(x, cols - 1, 0))
    dst[row, :, 0:128] = left.astype(BF16)
    dst[row, :, 128:256] = x.astype(BF16)
    dst[row, :, 256:384] = right.astype(BF16)


def lanes(x):
    return jnp.concatenate([x[i : i + 1] for i in range(4)], axis=1)


def prepare_kernel(scale_ref, img_ref, w1_ref, pix_ref, frac_ref, acc, weights, blends, x1):
    for i in range(4):
        put_columns(x1, i, img_ref[i].astype(F32))
    own = x1[...].reshape(1024, 384)
    acc[0:512] = jnp.zeros((512, 128), F32)
    acc[1536:1792] = jnp.zeros((256, 128), F32)
    acc[512:1536] = dot(own, w1_ref[0])
    acc[256:1280] += dot(own, w1_ref[1])
    acc[0:1024] += dot(own, w1_ref[2])
    scale = scale_ref[0]
    col_iota = lax.broadcasted_iota(jnp.int32, (256, 512), 0)
    row_iota = lax.broadcasted_iota(jnp.int32, (8, 512), 0)
    for k in range(8):
        pix = lanes(pix_ref[4 * k : 4 * k + 4])
        fr = lanes(frac_ref[0, 4 * k : 4 * k + 4])
        fc = lanes(frac_ref[1, 4 * k : 4 * k + 4])
        col = pix & 255
        row = pix >> 8
        weights[k] = jnp.where(
            col_iota == col, 1.0 - fc, jnp.where(col_iota == col + 1, fc, 0.0)
        ).astype(BF16)
        blends[k] = scale * jnp.where(
            row_iota == row, 1.0 - fr, jnp.where(row_iota == row + 1, fr, 0.0)
        )


def prepare(scale, img, w1, pix, frac):
    return pl.pallas_call(
        prepare_kernel,
        out_shape=(
            jax.ShapeDtypeStruct((1792, 128), F32),
            jax.ShapeDtypeStruct((8, 256, 512), BF16),
            jax.ShapeDtypeStruct((8, 8, 512), F32),
        ),
        in_specs=[whole(pltpu.SMEM)] + [whole(pltpu.VMEM)] * 4,
        out_specs=(whole(pltpu.VMEM),) * 3,
        scratch_shapes=[pltpu.VMEM((4, 256, 384), BF16)],
        compiler_params=pltpu.CompilerParams(vmem_limit_bytes=24 * 2**20),
        cost_estimate=pl.CostEstimate(flops=10**9, bytes_accessed=4 * 10**6, transcendentals=0),
        name="prepare",
    )(scale, img, w1, pix, frac)


def features_kernel(
    pos_ref, far_ref, core_ref, w1_ref, w2_ref, wr_ref, part_ref, weights, blends, out_ref,
    x1, x2, acc, packed,
):
    slab = pos_ref[0]
    even = (1 - slab % 2).astype(F32)
    odd = 1.0 - even
    not_first = jnp.where(slab == 0, 0.0, 1.0)
    not_last = jnp.where(slab == 3, 0.0, 1.0)
    for i in range(2):
        row = even * far_ref[1 + i].astype(F32) + odd * core_ref[1 + i].astype(F32)
        put_columns(x1, i, row)
    for i in range(3):
        row = even * core_ref[i].astype(F32) + odd * far_ref[i].astype(F32)
        put_columns(x1, 2 + i, row)
    head = dot(x1[0:2].reshape(512, 384), w1_ref[0])
    head0 = head[0:256] + dot(x1[1], w1_ref[1])
    tail0 = dot(x1[2:3].reshape(256, 384), w1_ref[0])
    tail1 = dot(x1[2:4].reshape(512, 384), w1_ref[1])
    tail2 = dot(x1[2:5].reshape(768, 384), w1_ref[2])
    for i in range(7):
        h = part_ref[i * 256 : (i + 1) * 256]
        if i == 0:
            h = h + head0
        elif i == 1:
            h = h + head[256:512]
        elif i == 4:
            h = h + tail2[0:256]
        elif i == 5:
            h = h + tail2[256:512] + tail1[0:256]
        elif i == 6:
            h = h + tail2[512:768] + tail1[256:512] + tail0
        h = jnp.maximum(h, 0.0)
        if i == 0:
            h = h * not_first
        if i >= 5:
            h = h * not_last
        put_columns(x2, i, h)
    acc[...] = dot(x2[0:5].reshape(1280, 384), w2_ref[0])
    acc[...] += dot(x2[1:6].reshape(1280, 384), w2_ref[1])
    acc[...] += dot(x2[2:7].reshape(1280, 384), w2_ref[2])
    table = []
    for i in range(5):
        h = jnp.maximum(acc[i * 256 : (i + 1) * 256], 0.0)
        if i == 4:
            h = h * not_last
        table.append(dot_nt(wr_ref[...], h.astype(BF16)))
    table = jnp.concatenate(table, axis=0).astype(BF16)
    for k in range(8):
        got = dot(table, weights[k])
        blend = blends[k]
        total = got[0:32] * blend[0:1]
        for r in range(1, 5):
            total = total + got[32 * r : 32 * r + 32] * blend[r : r + 1]
        block = jnp.concatenate([total[:, 128 * i : 128 * i + 128] for i in range(4)], axis=0)
        packed[pl.ds(k, 128, stride=8), :] = block.T
    out_ref[...] = packed[...].astype(BF16)


def features(slab, far, core, w1, w2, wr, part, weights, blends):
    return pl.pallas_call(
        features_kernel,
        out_shape=jax.ShapeDtypeStruct((1024, 128), BF16),
        in_specs=[whole(pltpu.SMEM)] + [whole(pltpu.VMEM)] * 8,
        out_specs=whole(pltpu.VMEM),
        scratch_shapes=[
            pltpu.VMEM((5, 256, 384), BF16),
            pltpu.VMEM((7, 256, 384), BF16),
            pltpu.VMEM((1280, 128), F32),
            pltpu.VMEM((1024, 128), F32),
        ],
        compiler_params=pltpu.CompilerParams(vmem_limit_bytes=32 * 2**20),
        name="features",
    )(slab, far, core, w1, w2, wr, part, weights, blends)


def scatter_kernel(val_ref, by_lane_ref, by_row_ref, out_ref):
    val = val_ref[...]
    lo_iota = lax.broadcasted_iota(jnp.int32, (256, 1024), 0)
    hi_iota = lax.broadcasted_iota(jnp.int32, (1024, 128), 1) // 32
    sel_row = lax.broadcasted_iota(jnp.int32, (128, 128), 0)
    sel_col = lax.broadcasted_iota(jnp.int32, (128, 128), 1) % 32
    total = jnp.zeros((256, 128), F32)
    for s in range(4):
        one_hot = jnp.where(lo_iota == (by_lane_ref[s : s + 1] >> 2), 1.0, 0.0).astype(BF16)
        select = jnp.where(sel_row == sel_col + 32 * s, 1.0, 0.0).astype(BF16)
        spread = dot(val, select)
        hi = by_row_ref[:, s : s + 1] & 3
        spread = jnp.where(hi_iota == hi, spread, 0.0).astype(BF16)
        total = total + dot(one_hot, spread)
    out_ref[...] = total.reshape(2, 128, 128).astype(BF16)


def scatter(val, by_lane, by_row):
    return pl.pallas_call(
        scatter_kernel,
        out_shape=jax.ShapeDtypeStruct((2, 128, 128), BF16),
        in_specs=[whole(pltpu.VMEM)] * 3,
        out_specs=whole(pltpu.VMEM),
        compiler_params=pltpu.CompilerParams(vmem_limit_bytes=40 * 2**20),
        name="scatter",
    )(val, by_lane, by_row)


def put_depth(dst, plane, x):
    step = lax.broadcasted_iota(jnp.int32, x.shape, 0) % 16
    lane = lax.broadcasted_iota(jnp.int32, x.shape, 1)
    rows = x.shape[0]
    before = jnp.where(step == 0, 0.0, pltpu.roll(x, 1, 0))
    after = jnp.where(step == 15, 0.0, pltpu.roll(x, rows - 1, 0))
    side = pltpu.roll(jnp.where(lane >= 96, before, after), 32, 1)
    dst[plane, :, 0:128] = x.astype(BF16)
    dst[plane, :, 128:256] = jnp.where(lane < 64, side, 0.0).astype(BF16)


def volume_start_kernel(own_ref, w_ref, acc, x1):
    for i in range(2):
        put_depth(x1, i, own_ref[i].astype(F32))
    zero = jnp.zeros((160, 128), F32)
    acc[0:160] = zero
    acc[480:640] = zero
    for k, dx in enumerate((1, 0, 2)):
        total = None
        for dy in range(3):
            rows = x1[:, dy * 16 : dy * 16 + 160, :].reshape(320, 256)
            part = dot_nt(rows, w_ref[dx * 3 + dy])
            total = part if total is None else total + part
        at = (2 - dx) * 160
        if k == 0:
            acc[at : at + 320] = total
        else:
            acc[at : at + 320] += total


def volume_start(own, w1):
    return pl.pallas_call(
        volume_start_kernel,
        out_shape=jax.ShapeDtypeStruct((640, 128), F32),
        in_specs=[whole(pltpu.VMEM)] * 2,
        out_specs=whole(pltpu.VMEM),
        scratch_shapes=[pltpu.VMEM((2, 192, 256), BF16)],
        compiler_params=pltpu.CompilerParams(vmem_limit_bytes=16 * 2**20),
        name="volume_start",
    )(own, w1)


def volume_kernel(
    pos_ref, own_ref, next_ref, near_ref, part_ref, w1_ref, w2_ref, out_ref, x1, x2, acc
):
    p = pos_ref[0]
    q = pos_ref[1]
    even = (1 - p % 2).astype(F32)
    odd = 1.0 - even
    for i in range(2):
        near = near_ref[i].astype(F32)
        nxt = next_ref[i].astype(F32)
        put_depth(x1, i, even * nxt + odd * near)
        put_depth(x1, 2 + i, even * near + odd * nxt)
    sums = [part_ref[i * 160 : (i + 1) * 160] for i in range(4)]
    for dy in range(3):
        rows = slice(dy * 16, dy * 16 + 160)
        low0 = dot_nt(x1[0:2, rows, :].reshape(320, 256), w1_ref[dy])
        low1 = dot_nt(x1[1, rows, :], w1_ref[3 + dy])
        high1 = dot_nt(x1[2, rows, :], w1_ref[3 + dy])
        high2 = dot_nt(x1[2:4, rows, :].reshape(320, 256), w1_ref[6 + dy])
        sums[0] = sums[0] + low0[0:160] + low1
        sums[1] = sums[1] + low0[160:320]
        sums[2] = sums[2] + high2[0:160]
        sums[3] = sums[3] + high2[160:320] + high1
    y = lax.broadcasted_iota(jnp.int32, (160, 128), 0) // 16
    first_y = jnp.where(q == 0, 1, 0)
    last_y = jnp.where(q == 3, 8, 9)
    inside = (y >= first_y) & (y <= last_y)
    for i in range(4):
        h = jnp.where(inside, jnp.maximum(sums[i], 0.0), 0.0)
        if i == 0:
            h = h * jnp.where(p == 0, 0.0, 1.0)
        if i == 3:
            h = h * jnp.where(p == 31, 0.0, 1.0)
        put_depth(x2, i, h)
    for t in range(9):
        dx, dy = divmod(t, 3)
        part = dot_nt(x2[dx : dx + 2, dy * 16 : dy * 16 + 128, :].reshape(256, 256), w2_ref[t])
        if t == 0:
            acc[...] = part
        else:
            acc[...] += part
    place_row = lax.broadcasted_iota(jnp.int32, (128, 512), 0) * 4
    place_col = lax.broadcasted_iota(jnp.int32, (128, 512), 1)
    both = []
    for i in range(2):
        res = acc[i * 128 : (i + 1) * 128] + own_ref[i, 32:160].astype(F32)
        both.append(res.T.astype(BF16))
    total = [None, None]
    for z in range(4):
        place = jnp.where(place_col == place_row + z, 1.0, 0.0).astype(BF16)
        rows = jnp.concatenate([b[32 * z : 32 * z + 32] for b in both], axis=0)
        part = dot(rows, place)
        total = part if z == 0 else total + part
    for i in range(2):
        out_ref[:, 512 * i : 512 * i + 512] = total[32 * i : 32 * i + 32].astype(BF16)


def volume_convs(pos, own, nxt, near, part, w1, w2):
    return pl.pallas_call(
        volume_kernel,
        out_shape=jax.ShapeDtypeStruct((32, 1024), BF16),
        in_specs=[whole(pltpu.SMEM)] + [whole(pltpu.VMEM)] * 6,
        out_specs=whole(pltpu.VMEM),
        scratch_shapes=[
            pltpu.VMEM((4, 192, 256), BF16),
            pltpu.VMEM((4, 160, 256), BF16),
            pltpu.VMEM((256, 128), F32),
        ],
        compiler_params=pltpu.CompilerParams(vmem_limit_bytes=32 * 2**20),
        name="volume",
    )(pos, own, nxt, near, part, w1, w2)


def banded(weight):
    taps = weight.reshape(9, 3, 32, 32)
    zero = jnp.zeros((9, 32, 32), weight.dtype)
    rows = []
    for z in range(4):
        blocks = [zero] * 8
        for dz in range(3):
            at = z + dz - 1
            blocks[4 if at < 0 else 5 if at > 3 else at] = taps[:, dz]
        rows.append(jnp.concatenate(blocks, axis=2))
    return jnp.concatenate(rows, axis=1)


def swap(x, partner, cams, slabs):
    pairs = []
    for p in range(cams):
        for s in range(slabs):
            to = partner(p, s)
            if 0 <= to[0] < cams and 0 <= to[1] < slabs:
                pairs.append((p * slabs + s, to[0] * slabs + to[1]))
    return lax.ppermute(x, AXES, pairs)


def core_partner(p, s):
    return p, s ^ 1


def far_partner(p, s):
    return p, (s + 1 if s % 2 else s - 1)


def near_partner(p, s):
    return p ^ 1, s


def next_partner(p, s):
    return (p + 1 if p % 2 else p - 1), s


def local(
    image,
    w_first,
    w_second,
    w_reduce,
    cam_weight,
    sample_pixel,
    sample_frac,
    voxel_slot,
    wv_first,
    wv_second,
):
    cams = lax.axis_size("cam")
    slabs = lax.axis_size("slab")
    p = lax.axis_index("cam")
    s = lax.axis_index("slab")
    even = s % 2 == 0
    img = image[0]
    top, bottom = img[0:3], img[1:4]
    far = swap(jnp.where(even, top, bottom), far_partner, cams, slabs)
    core = swap(jnp.where(even, bottom, top), core_partner, cams, slabs)

    pix = sample_pixel[0].T
    frac = jnp.transpose(sample_frac[0], (0, 2, 1))
    w1 = w_first.reshape(3, 384, 128)
    w2 = w_second.reshape(3, 384, 128)
    by_row = voxel_slot[0].reshape(1024, 4)
    by_lane = by_row.T
    band1 = banded(wv_first)
    band2 = banded(wv_second)
    slab_pos = s.astype(jnp.int32).reshape(1)

    part, weights, blends = prepare(cam_weight, img, w1, pix, frac)
    sent = features(slab_pos, far, core, w1, w2, w_reduce.T, part, weights, blends)
    got = lax.all_to_all(sent.reshape(128, 8, 128), AXES, 0, 0, tiled=True).reshape(1024, 128)
    volume = scatter(got, by_lane, by_row)

    pos = jnp.stack([p, s]).astype(jnp.int32)
    top, bottom = volume[:, 0:32], volume[:, 96:128]
    far = swap(jnp.where(even, top, bottom), far_partner, cams, slabs)
    core = swap(jnp.where(even, bottom, top), core_partner, cams, slabs)
    above = jnp.where(even, far, core)
    below = jnp.where(even, core, far)
    own = jnp.concatenate([above, volume, below], axis=1)
    nxt = swap(own, next_partner, cams, slabs)
    near = swap(own, near_partner, cams, slabs)
    part = volume_start(own, band1)
    out = volume_convs(pos, own, nxt, near, part, band1, band2)
    return out.reshape(32, 2, 512)


def solution(mesh):
    placed = (
        P(("dp", "cam"), "slab", None, None),
        P(),
        P(),
        P(),
        P("cam"),
        P(("dp", "cam", "slab"), None, None),
        P(("dp", "cam", "slab"), None, None, None),
        P(("dp", "cam", "slab"), None, None),
        P(),
        P(),
    )
    return jax.shard_map(
        local, mesh=mesh, in_specs=placed, out_specs=P(None, ("dp", "cam"), "slab"), check_vma=False
    )
```

```python
import jax
import jax.numpy as jnp
from jax import lax
from jax.experimental import pallas as pl
from jax.experimental.pallas import tpu as pltpu
from jax.sharding import PartitionSpec as P

AXES = ("cam", "slab")
F32 = jnp.float32
BF16 = jnp.bfloat16


def dot(a, b):
    return jnp.dot(a, b, preferred_element_type=F32)


def dot_nt(a, b):
    return lax.dot_general(a, b, (((1,), (1,)), ((), ())), preferred_element_type=F32)


def whole(memory_space):
    return pl.BlockSpec(memory_space=memory_space)


def put_columns(dst, row, x):
    cols = x.shape[0]
    pos = lax.broadcasted_iota(jnp.int32, x.shape, 0)
    left = jnp.where(pos == 0, 0.0, pltpu.roll(x, 1, 0))
    right = jnp.where(pos == cols - 1, 0.0, pltpu.roll(x, cols - 1, 0))
    dst[row, :, 0:128] = left.astype(BF16)
    dst[row, :, 128:256] = x.astype(BF16)
    dst[row, :, 256:384] = right.astype(BF16)


def lanes(x):
    return jnp.concatenate([x[i : i + 1] for i in range(4)], axis=1)


def sample_weights(scale_ref, pix_ref, frac_ref, weights, blends):
    scale = scale_ref[0]
    col_iota = lax.broadcasted_iota(jnp.int32, (256, 512), 0)
    row_iota = lax.broadcasted_iota(jnp.int32, (8, 512), 0)
    for k in range(8):
        pix = lanes(pix_ref[4 * k : 4 * k + 4])
        fr = lanes(frac_ref[0, 4 * k : 4 * k + 4])
        fc = lanes(frac_ref[1, 4 * k : 4 * k + 4])
        col = pix & 255
        row = pix >> 8
        weights[k] = jnp.where(
            col_iota == col, 1.0 - fc, jnp.where(col_iota == col + 1, fc, 0.0)
        ).astype(BF16)
        blends[k] = scale * jnp.where(
            row_iota == row, 1.0 - fr, jnp.where(row_iota == row + 1, fr, 0.0)
        )


def prepare_kernel(
    scale_ref, img_hbm, w1_hbm, pix_hbm, frac_hbm, acc, weights, blends,
    x1, img_ref, w1_ref, pix_ref, frac_ref, sems,
):
    pairs = ((pix_hbm, pix_ref), (frac_hbm, frac_ref), (img_hbm, img_ref), (w1_hbm, w1_ref))
    copies = [pltpu.make_async_copy(src, dst, sems.at[i]) for i, (src, dst) in enumerate(pairs)]
    for copy in copies:
        copy.start()
    copies[0].wait()
    copies[1].wait()
    sample_weights(scale_ref, pix_ref, frac_ref, weights, blends)
    copies[2].wait()
    copies[3].wait()
    for i in range(4):
        put_columns(x1, i, img_ref[i].astype(F32))
    own = x1[...].reshape(1024, 384)
    acc[0:512] = jnp.zeros((512, 128), F32)
    acc[1536:1792] = jnp.zeros((256, 128), F32)
    acc[512:1536] = dot(own, w1_ref[0])
    acc[256:1280] += dot(own, w1_ref[1])
    acc[0:1024] += dot(own, w1_ref[2])


def prepare(scale, img, w1, pix, frac):
    return pl.pallas_call(
        prepare_kernel,
        out_shape=(
            jax.ShapeDtypeStruct((1792, 128), F32),
            jax.ShapeDtypeStruct((8, 256, 512), BF16),
            jax.ShapeDtypeStruct((8, 8, 512), F32),
        ),
        in_specs=[whole(pltpu.SMEM)] + [whole(pltpu.HBM)] * 4,
        out_specs=(whole(pltpu.VMEM),) * 3,
        scratch_shapes=[
            pltpu.VMEM((4, 256, 384), BF16),
            pltpu.VMEM((4, 256, 128), BF16),
            pltpu.VMEM((3, 384, 128), BF16),
            pltpu.VMEM((32, 128), jnp.int32),
            pltpu.VMEM((2, 32, 128), F32),
            pltpu.SemaphoreType.DMA((4,)),
        ],
        compiler_params=pltpu.CompilerParams(vmem_limit_bytes=24 * 2**20),
        cost_estimate=pl.CostEstimate(flops=10**9, bytes_accessed=4 * 10**6, transcendentals=0),
        name="prepare",
    )(scale, *(pltpu.with_memory_space_constraint(x, pltpu.HBM) for x in (img, w1, pix, frac)))


def features_kernel(
    pos_ref, far_ref, core_ref, w1_ref, w2_ref, wr_ref, part_ref, weights, blends, out_ref,
    x1, x2, acc, packed,
):
    slab = pos_ref[0]
    even = (1 - slab % 2).astype(F32)
    odd = 1.0 - even
    not_first = jnp.where(slab == 0, 0.0, 1.0)
    not_last = jnp.where(slab == 3, 0.0, 1.0)
    for i in range(2):
        row = even * far_ref[1 + i].astype(F32) + odd * core_ref[1 + i].astype(F32)
        put_columns(x1, i, row)
    for i in range(3):
        row = even * core_ref[i].astype(F32) + odd * far_ref[i].astype(F32)
        put_columns(x1, 2 + i, row)
    head = dot(x1[0:2].reshape(512, 384), w1_ref[0])
    head0 = head[0:256] + dot(x1[1], w1_ref[1])
    tail0 = dot(x1[2:3].reshape(256, 384), w1_ref[0])
    tail1 = dot(x1[2:4].reshape(512, 384), w1_ref[1])
    tail2 = dot(x1[2:5].reshape(768, 384), w1_ref[2])
    for i in range(7):
        h = part_ref[i * 256 : (i + 1) * 256]
        if i == 0:
            h = h + head0
        elif i == 1:
            h = h + head[256:512]
        elif i == 4:
            h = h + tail2[0:256]
        elif i == 5:
            h = h + tail2[256:512] + tail1[0:256]
        elif i == 6:
            h = h + tail2[512:768] + tail1[256:512] + tail0
        h = jnp.maximum(h, 0.0)
        if i == 0:
            h = h * not_first
        if i >= 5:
            h = h * not_last
        put_columns(x2, i, h)
    acc[...] = dot(x2[0:5].reshape(1280, 384), w2_ref[0])
    acc[...] += dot(x2[1:6].reshape(1280, 384), w2_ref[1])
    acc[...] += dot(x2[2:7].reshape(1280, 384), w2_ref[2])
    table = []
    for i in range(5):
        h = jnp.maximum(acc[i * 256 : (i + 1) * 256], 0.0)
        if i == 4:
            h = h * not_last
        table.append(dot_nt(wr_ref[...], h.astype(BF16)))
    table = jnp.concatenate(table, axis=0).astype(BF16)
    for k in range(8):
        got = dot(table, weights[k])
        blend = blends[k]
        total = got[0:32] * blend[0:1]
        for r in range(1, 5):
            total = total + got[32 * r : 32 * r + 32] * blend[r : r + 1]
        block = jnp.concatenate([total[:, 128 * i : 128 * i + 128] for i in range(4)], axis=0)
        packed[pl.ds(k, 128, stride=8), :] = block.T
    out_ref[...] = packed[...].astype(BF16)


def features(slab, far, core, w1, w2, wr, part, weights, blends):
    return pl.pallas_call(
        features_kernel,
        out_shape=jax.ShapeDtypeStruct((1024, 128), BF16),
        in_specs=[whole(pltpu.SMEM)] + [whole(pltpu.VMEM)] * 8,
        out_specs=whole(pltpu.VMEM),
        scratch_shapes=[
            pltpu.VMEM((5, 256, 384), BF16),
            pltpu.VMEM((7, 256, 384), BF16),
            pltpu.VMEM((1280, 128), F32),
            pltpu.VMEM((1024, 128), F32),
        ],
        compiler_params=pltpu.CompilerParams(vmem_limit_bytes=32 * 2**20),
        name="features",
    )(slab, far, core, w1, w2, wr, part, weights, blends)


def slots_kernel(by_lane_ref, one_hot):
    lo_iota = lax.broadcasted_iota(jnp.int32, (256, 1024), 0)
    for s in range(4):
        hit = lo_iota == (by_lane_ref[s : s + 1] >> 2)
        one_hot[:, 1024 * s : 1024 * s + 1024] = jnp.where(hit, 1.0, 0.0).astype(BF16)


def slots(by_lane):
    return pl.pallas_call(
        slots_kernel,
        out_shape=jax.ShapeDtypeStruct((256, 4096), BF16),
        in_specs=[whole(pltpu.VMEM)],
        out_specs=whole(pltpu.VMEM),
        compiler_params=pltpu.CompilerParams(vmem_limit_bytes=16 * 2**20),
        cost_estimate=pl.CostEstimate(flops=10**7, bytes_accessed=2 * 10**6, transcendentals=0),
        name="slots",
    )(by_lane)


def spread_kernel(pos_ref, val_ref, one_hot, by_row_ref, spread, facing):
    start = pl.multiple_of((pos_ref[0] % 2) * 96, 32)
    val = val_ref[...]
    hi_iota = lax.broadcasted_iota(jnp.int32, (1024, 128), 1) // 32
    sel_row = lax.broadcasted_iota(jnp.int32, (128, 128), 0)
    sel_col = lax.broadcasted_iota(jnp.int32, (128, 128), 1) % 32
    for s in range(4):
        select = jnp.where(sel_row == sel_col + 32 * s, 1.0, 0.0).astype(BF16)
        block = hi_iota == (by_row_ref[:, s : s + 1] & 3)
        spread[1024 * s : 1024 * s + 1024] = jnp.where(block, dot(val, select), 0.0).astype(BF16)
    for i in range(2):
        rows = one_hot[pl.ds(128 * i + start, 32), :]
        facing[i] = dot(rows, spread[...]).astype(BF16)


def spread_values(slab, val, one_hot, by_row):
    return pl.pallas_call(
        spread_kernel,
        out_shape=(
            jax.ShapeDtypeStruct((4096, 128), BF16),
            jax.ShapeDtypeStruct((2, 32, 128), BF16),
        ),
        in_specs=[whole(pltpu.SMEM)] + [whole(pltpu.VMEM)] * 3,
        out_specs=(whole(pltpu.VMEM),) * 2,
        compiler_params=pltpu.CompilerParams(vmem_limit_bytes=16 * 2**20),
        name="spread",
    )(slab, val, one_hot, by_row)


def scatter_kernel(one_hot, spread, out_ref):
    out_ref[...] = dot(one_hot[...], spread[...]).reshape(2, 128, 128).astype(BF16)


def scatter(one_hot, spread):
    return pl.pallas_call(
        scatter_kernel,
        out_shape=jax.ShapeDtypeStruct((2, 128, 128), BF16),
        in_specs=[whole(pltpu.VMEM)] * 2,
        out_specs=whole(pltpu.VMEM),
        compiler_params=pltpu.CompilerParams(vmem_limit_bytes=16 * 2**20),
        cost_estimate=pl.CostEstimate(flops=3 * 10**8, bytes_accessed=3 * 10**6, transcendentals=0),
        name="scatter",
    )(one_hot, spread)


def put_depth(dst, plane, x):
    step = lax.broadcasted_iota(jnp.int32, x.shape, 0) % 16
    lane = lax.broadcasted_iota(jnp.int32, x.shape, 1)
    rows = x.shape[0]
    before = jnp.where(step == 0, 0.0, pltpu.roll(x, 1, 0))
    after = jnp.where(step == 15, 0.0, pltpu.roll(x, rows - 1, 0))
    side = pltpu.roll(jnp.where(lane >= 96, before, after), 32, 1)
    dst[plane, :, 0:128] = x.astype(BF16)
    dst[plane, :, 128:256] = jnp.where(lane < 64, side, 0.0).astype(BF16)


def volume_start_kernel(own_ref, w_ref, acc, x1):
    for i in range(2):
        put_depth(x1, i, own_ref[i].astype(F32))
    zero = jnp.zeros((160, 128), F32)
    acc[0:160] = zero
    acc[480:640] = zero
    for k, dx in enumerate((1, 0, 2)):
        total = None
        for dy in range(3):
            rows = x1[:, dy * 16 : dy * 16 + 160, :].reshape(320, 256)
            part = dot_nt(rows, w_ref[dx * 3 + dy])
            total = part if total is None else total + part
        at = (2 - dx) * 160
        if k == 0:
            acc[at : at + 320] = total
        else:
            acc[at : at + 320] += total


def volume_start(own, w1):
    return pl.pallas_call(
        volume_start_kernel,
        out_shape=jax.ShapeDtypeStruct((640, 128), F32),
        in_specs=[whole(pltpu.VMEM)] * 2,
        out_specs=whole(pltpu.VMEM),
        scratch_shapes=[pltpu.VMEM((2, 192, 256), BF16)],
        compiler_params=pltpu.CompilerParams(vmem_limit_bytes=16 * 2**20),
        name="volume_start",
    )(own, w1)


def volume_kernel(
    pos_ref, own_ref, next_ref, near_ref, part_ref, w1_ref, w2_ref, out_ref, x1, x2, acc, packed
):
    p = pos_ref[0]
    q = pos_ref[1]
    even = (1 - p % 2).astype(F32)
    odd = 1.0 - even
    for i in range(2):
        near = near_ref[i].astype(F32)
        nxt = next_ref[i].astype(F32)
        put_depth(x1, i, even * nxt + odd * near)
        put_depth(x1, 2 + i, even * near + odd * nxt)
    sums = [part_ref[i * 160 : (i + 1) * 160] for i in range(4)]
    for dy in range(3):
        rows = slice(dy * 16, dy * 16 + 160)
        low0 = dot_nt(x1[0:2, rows, :].reshape(320, 256), w1_ref[dy])
        low1 = dot_nt(x1[1, rows, :], w1_ref[3 + dy])
        high1 = dot_nt(x1[2, rows, :], w1_ref[3 + dy])
        high2 = dot_nt(x1[2:4, rows, :].reshape(320, 256), w1_ref[6 + dy])
        sums[0] = sums[0] + low0[0:160] + low1
        sums[1] = sums[1] + low0[160:320]
        sums[2] = sums[2] + high2[0:160]
        sums[3] = sums[3] + high2[160:320] + high1
    y = lax.broadcasted_iota(jnp.int32, (160, 128), 0) // 16
    first_y = jnp.where(q == 0, 1, 0)
    last_y = jnp.where(q == 3, 8, 9)
    inside = (y >= first_y) & (y <= last_y)
    for i in range(4):
        h = jnp.where(inside, jnp.maximum(sums[i], 0.0), 0.0)
        if i == 0:
            h = h * jnp.where(p == 0, 0.0, 1.0)
        if i == 3:
            h = h * jnp.where(p == 31, 0.0, 1.0)
        put_depth(x2, i, h)
    for t in range(9):
        dx, dy = divmod(t, 3)
        part = dot_nt(x2[dx : dx + 2, dy * 16 : dy * 16 + 128, :].reshape(256, 256), w2_ref[t])
        if t == 0:
            acc[...] = part
        else:
            acc[...] += part
    for i in range(2):
        res = acc[i * 128 : (i + 1) * 128] + own_ref[i, 32:160].astype(F32)
        res = res.T
        for k in range(4):
            block = [res[32 * z : 32 * z + 32, 32 * k : 32 * k + 32] for z in range(4)]
            packed[pl.ds(2 * k + i, 32, stride=8), :] = jnp.concatenate(block, axis=1)
    source = lax.broadcasted_iota(jnp.int32, (128, 128), 0)
    target = lax.broadcasted_iota(jnp.int32, (128, 128), 1)
    place = jnp.where(target == (source % 32) * 4 + source // 32, 1.0, 0.0).astype(BF16)
    out_ref[...] = dot(packed[...].astype(BF16), place).astype(BF16)


def volume_convs(pos, own, nxt, near, part, w1, w2):
    return pl.pallas_call(
        volume_kernel,
        out_shape=jax.ShapeDtypeStruct((256, 128), BF16),
        in_specs=[whole(pltpu.SMEM)] + [whole(pltpu.VMEM)] * 6,
        out_specs=whole(pltpu.VMEM),
        scratch_shapes=[
            pltpu.VMEM((4, 192, 256), BF16),
            pltpu.VMEM((4, 160, 256), BF16),
            pltpu.VMEM((256, 128), F32),
            pltpu.VMEM((256, 128), F32),
        ],
        compiler_params=pltpu.CompilerParams(vmem_limit_bytes=32 * 2**20),
        name="volume",
    )(pos, own, nxt, near, part, w1, w2)


def banded(weight):
    taps = weight.reshape(9, 3, 32, 32)
    zero = jnp.zeros((9, 32, 32), weight.dtype)
    rows = []
    for z in range(4):
        blocks = [zero] * 8
        for dz in range(3):
            at = z + dz - 1
            blocks[4 if at < 0 else 5 if at > 3 else at] = taps[:, dz]
        rows.append(jnp.concatenate(blocks, axis=2))
    return jnp.concatenate(rows, axis=1)


def swap(x, partner, cams, slabs):
    pairs = []
    for p in range(cams):
        for s in range(slabs):
            to = partner(p, s)
            if 0 <= to[0] < cams and 0 <= to[1] < slabs:
                pairs.append((p * slabs + s, to[0] * slabs + to[1]))
    return lax.ppermute(x, AXES, pairs)


def core_partner(p, s):
    return p, s ^ 1


def far_partner(p, s):
    return p, (s + 1 if s % 2 else s - 1)


def near_partner(p, s):
    return p ^ 1, s


def next_partner(p, s):
    return (p + 1 if p % 2 else p - 1), s


def local(
    image,
    w_first,
    w_second,
    w_reduce,
    cam_weight,
    sample_pixel,
    sample_frac,
    voxel_slot,
    wv_first,
    wv_second,
):
    cams = lax.axis_size("cam")
    slabs = lax.axis_size("slab")
    p = lax.axis_index("cam")
    s = lax.axis_index("slab")
    even = s % 2 == 0
    img = image[0]
    top, bottom = img[0:3], img[1:4]
    far = swap(jnp.where(even, top, bottom), far_partner, cams, slabs)
    core = swap(jnp.where(even, bottom, top), core_partner, cams, slabs)

    pix = sample_pixel[0].T
    frac = jnp.transpose(sample_frac[0], (0, 2, 1))
    w1 = w_first.reshape(3, 384, 128)
    w2 = w_second.reshape(3, 384, 128)
    by_row = voxel_slot[0].reshape(1024, 4)
    by_lane = by_row.T
    band1 = banded(wv_first)
    band2 = banded(wv_second)
    slab_pos = s.astype(jnp.int32).reshape(1)

    part, weights, blends = prepare(cam_weight, img, w1, pix, frac)
    sent = features(slab_pos, far, core, w1, w2, w_reduce.T, part, weights, blends)
    got = lax.all_to_all(sent.reshape(128, 8, 128), AXES, 0, 0, tiled=True).reshape(1024, 128)
    one_hot = slots(by_lane)
    spread, facing = spread_values(slab_pos, got, one_hot, by_row)
    far = swap(facing, far_partner, cams, slabs)
    volume = scatter(one_hot, spread)

    pos = jnp.stack([p, s]).astype(jnp.int32)
    top, bottom = volume[:, 0:32], volume[:, 96:128]
    core = swap(jnp.where(even, bottom, top), core_partner, cams, slabs)
    above = jnp.where(even, far, core)
    below = jnp.where(even, core, far)
    own = jnp.concatenate([above, volume, below], axis=1)
    nxt = swap(own, next_partner, cams, slabs)
    near = swap(own, near_partner, cams, slabs)
    part = volume_start(own, band1)
    out = volume_convs(pos, own, nxt, near, part, band1, band2)
    return out.reshape(32, 4, 2, 128).transpose(0, 2, 1, 3).reshape(32, 2, 512)


def solution(mesh):
    placed = (
        P(("dp", "cam"), "slab", None, None),
        P(),
        P(),
        P(),
        P("cam"),
        P(("dp", "cam", "slab"), None, None),
        P(("dp", "cam", "slab"), None, None, None),
        P(("dp", "cam", "slab"), None, None),
        P(),
        P(),
    )
    return jax.shard_map(
        local, mesh=mesh, in_specs=placed, out_specs=P(None, ("dp", "cam"), "slab"), check_vma=False
    )
```

```python
import jax
import jax.numpy as jnp
from jax import lax
from jax.experimental import pallas as pl
from jax.experimental.pallas import tpu as pltpu
from jax.sharding import PartitionSpec as P

AXES = ("cam", "slab")
F32 = jnp.float32
BF16 = jnp.bfloat16


def dot(a, b):
    return jnp.dot(a, b, preferred_element_type=F32)


def dot_nt(a, b):
    return lax.dot_general(a, b, (((1,), (1,)), ((), ())), preferred_element_type=F32)


def whole(memory_space):
    return pl.BlockSpec(memory_space=memory_space)


def put_columns(dst, row, x):
    cols = x.shape[0]
    pos = lax.broadcasted_iota(jnp.int32, x.shape, 0)
    left = jnp.where(pos == 0, 0.0, pltpu.roll(x, 1, 0))
    right = jnp.where(pos == cols - 1, 0.0, pltpu.roll(x, cols - 1, 0))
    dst[row, :, 0:128] = left.astype(BF16)
    dst[row, :, 128:256] = x.astype(BF16)
    dst[row, :, 256:384] = right.astype(BF16)


def lanes(x):
    return jnp.concatenate([x[i : i + 1] for i in range(4)], axis=1)


def sample_weights(scale_ref, pix_ref, frac_ref, weights, blends):
    scale = scale_ref[0]
    col_iota = lax.broadcasted_iota(jnp.int32, (256, 512), 0)
    row_iota = lax.broadcasted_iota(jnp.int32, (8, 512), 0)
    for k in range(8):
        pix = lanes(pix_ref[4 * k : 4 * k + 4])
        fr = lanes(frac_ref[0, 4 * k : 4 * k + 4])
        fc = lanes(frac_ref[1, 4 * k : 4 * k + 4])
        col = pix & 255
        row = pix >> 8
        weights[k] = jnp.where(
            col_iota == col, 1.0 - fc, jnp.where(col_iota == col + 1, fc, 0.0)
        ).astype(BF16)
        blends[k] = scale * jnp.where(
            row_iota == row, 1.0 - fr, jnp.where(row_iota == row + 1, fr, 0.0)
        )


def prepare_kernel(
    scale_ref, img_hbm, w1_hbm, pix_hbm, frac_hbm, acc, weights, blends,
    x1, img_ref, w1_ref, pix_ref, frac_ref, sems,
):
    pairs = ((pix_hbm, pix_ref), (frac_hbm, frac_ref), (img_hbm, img_ref), (w1_hbm, w1_ref))
    copies = [pltpu.make_async_copy(src, dst, sems.at[i]) for i, (src, dst) in enumerate(pairs)]
    for copy in copies:
        copy.start()
    copies[0].wait()
    copies[1].wait()
    sample_weights(scale_ref, pix_ref, frac_ref, weights, blends)
    copies[2].wait()
    copies[3].wait()
    for i in range(4):
        put_columns(x1, i, img_ref[i].astype(F32))
    own = x1[...].reshape(1024, 384)
    acc[0:512] = jnp.zeros((512, 128), F32)
    acc[1536:1792] = jnp.zeros((256, 128), F32)
    acc[512:1536] = dot(own, w1_ref[0])
    acc[256:1280] += dot(own, w1_ref[1])
    acc[0:1024] += dot(own, w1_ref[2])


def prepare(scale, img, w1, pix, frac):
    return pl.pallas_call(
        prepare_kernel,
        out_shape=(
            jax.ShapeDtypeStruct((1792, 128), F32),
            jax.ShapeDtypeStruct((8, 256, 512), BF16),
            jax.ShapeDtypeStruct((8, 8, 512), F32),
        ),
        in_specs=[whole(pltpu.SMEM)] + [whole(pltpu.HBM)] * 4,
        out_specs=(whole(pltpu.VMEM),) * 3,
        scratch_shapes=[
            pltpu.VMEM((4, 256, 384), BF16),
            pltpu.VMEM((4, 256, 128), BF16),
            pltpu.VMEM((3, 384, 128), BF16),
            pltpu.VMEM((32, 128), jnp.int32),
            pltpu.VMEM((2, 32, 128), F32),
            pltpu.SemaphoreType.DMA((4,)),
        ],
        compiler_params=pltpu.CompilerParams(vmem_limit_bytes=24 * 2**20),
        cost_estimate=pl.CostEstimate(flops=10000000000, bytes_accessed=4 * 10**6, transcendentals=0),
        name="prepare",
    )(scale, *(pltpu.with_memory_space_constraint(x, pltpu.HBM) for x in (img, w1, pix, frac)))


def table_rows(acc, at, count, wr):
    rows = []
    for i in range(at, at + count):
        h = jnp.maximum(acc[i * 256 : (i + 1) * 256], 0.0)
        rows.append(dot_nt(wr, h.astype(BF16)))
    return rows


def middle_kernel(pos_ref, core_ref, w1_ref, w2_ref, wr_ref, part_ref, inner, table, x1, x2, acc):
    @pl.when(pos_ref[0] % 2 == 0)
    def _():
        for i in range(3):
            put_columns(x1, i, core_ref[i].astype(F32))
        tail0 = dot(x1[0], w1_ref[0])
        tail1 = dot(x1[0:2].reshape(512, 384), w1_ref[1])
        tail2 = dot(x1[0:3].reshape(768, 384), w1_ref[2])
        for i in range(2, 7):
            h = part_ref[i * 256 : (i + 1) * 256]
            if i == 4:
                h = h + tail2[0:256]
            elif i == 5:
                h = h + tail2[256:512] + tail1[0:256]
            elif i == 6:
                h = h + tail2[512:768] + tail1[256:512] + tail0
            put_columns(x2, i - 2, jnp.maximum(h, 0.0))
        inner[...] = x2[0:2]
        acc[...] = dot(x2[0:3].reshape(768, 384), w2_ref[0])
        acc[...] += dot(x2[1:4].reshape(768, 384), w2_ref[1])
        acc[...] += dot(x2[2:5].reshape(768, 384), w2_ref[2])
        table[...] = jnp.concatenate(table_rows(acc, 0, 3, wr_ref[...]), axis=0).astype(BF16)


def middle(slab, core, w1, w2, wr, part):
    return pl.pallas_call(
        middle_kernel,
        out_shape=(
            jax.ShapeDtypeStruct((2, 256, 384), BF16),
            jax.ShapeDtypeStruct((96, 256), BF16),
        ),
        in_specs=[whole(pltpu.SMEM)] + [whole(pltpu.VMEM)] * 5,
        out_specs=(whole(pltpu.VMEM),) * 2,
        scratch_shapes=[
            pltpu.VMEM((3, 256, 384), BF16),
            pltpu.VMEM((5, 256, 384), BF16),
            pltpu.VMEM((768, 128), F32),
        ],
        compiler_params=pltpu.CompilerParams(vmem_limit_bytes=24 * 2**20),
        cost_estimate=pl.CostEstimate(flops=1000000, bytes_accessed=10**3, transcendentals=0),
        name="middle",
    )(slab, core, w1, w2, wr, part)


def features_kernel(
    pos_ref, far_ref, core_ref, w1_ref, w2_ref, wr_ref, part_ref, weights, blends,
    inner, ready, out_ref, x1, x2, acc, table, packed,
):
    slab = pos_ref[0]
    not_first = jnp.where(slab == 0, 0.0, 1.0)
    not_last = jnp.where(slab == 3, 0.0, 1.0)

    def first_rows(above):
        for i in range(2):
            put_columns(x1, i, above[1 + i].astype(F32))
        head = dot(x1[0:2].reshape(512, 384), w1_ref[0])
        return head[0:256] + dot(x1[1], w1_ref[1]), head[256:512]

    @pl.when(slab % 2 == 0)
    def _():
        head0, head1 = first_rows(far_ref)
        put_columns(x2, 0, jnp.maximum(part_ref[0:256] + head0, 0.0) * not_first)
        put_columns(x2, 1, jnp.maximum(part_ref[256:512] + head1, 0.0))
        x2[2:4] = inner[...]
        acc[0:512] = dot(x2[0:2].reshape(512, 384), w2_ref[0])
        acc[0:512] += dot(x2[1:3].reshape(512, 384), w2_ref[1])
        acc[0:512] += dot(x2[2:4].reshape(512, 384), w2_ref[2])
        table[0:64] = jnp.concatenate(table_rows(acc, 0, 2, wr_ref[...]), axis=0).astype(BF16)
        table[64:160] = ready[...]

    @pl.when(slab % 2 == 1)
    def _():
        head0, head1 = first_rows(core_ref)
        for i in range(3):
            put_columns(x1, 2 + i, far_ref[i].astype(F32))
        tail0 = dot(x1[2], w1_ref[0])
        tail1 = dot(x1[2:4].reshape(512, 384), w1_ref[1])
        tail2 = dot(x1[2:5].reshape(768, 384), w1_ref[2])
        for i in range(7):
            h = part_ref[i * 256 : (i + 1) * 256]
            if i == 0:
                h = h + head0
            elif i == 1:
                h = h + head1
            elif i == 4:
                h = h + tail2[0:256]
            elif i == 5:
                h = h + tail2[256:512] + tail1[0:256]
            elif i == 6:
                h = h + tail2[512:768] + tail1[256:512] + tail0
            h = jnp.maximum(h, 0.0)
            if i >= 5:
                h = h * not_last
            put_columns(x2, i, h)
        acc[...] = dot(x2[0:5].reshape(1280, 384), w2_ref[0])
        acc[...] += dot(x2[1:6].reshape(1280, 384), w2_ref[1])
        acc[...] += dot(x2[2:7].reshape(1280, 384), w2_ref[2])
        rows = table_rows(acc, 0, 5, wr_ref[...])
        rows[4] = rows[4] * not_last
        table[...] = jnp.concatenate(rows, axis=0).astype(BF16)

    for k in range(8):
        got = dot(table[...], weights[k])
        blend = blends[k]
        total = got[0:32] * blend[0:1]
        for r in range(1, 5):
            total = total + got[32 * r : 32 * r + 32] * blend[r : r + 1]
        block = jnp.concatenate([total[:, 128 * i : 128 * i + 128] for i in range(4)], axis=0)
        packed[pl.ds(k, 128, stride=8), :] = block.T
    out_ref[...] = packed[...].astype(BF16)


def features(slab, far, core, w1, w2, wr, part, weights, blends, inner, ready):
    return pl.pallas_call(
        features_kernel,
        out_shape=jax.ShapeDtypeStruct((1024, 128), BF16),
        in_specs=[whole(pltpu.SMEM)] + [whole(pltpu.VMEM)] * 10,
        out_specs=whole(pltpu.VMEM),
        scratch_shapes=[
            pltpu.VMEM((5, 256, 384), BF16),
            pltpu.VMEM((7, 256, 384), BF16),
            pltpu.VMEM((1280, 128), F32),
            pltpu.VMEM((160, 256), BF16),
            pltpu.VMEM((1024, 128), F32),
        ],
        compiler_params=pltpu.CompilerParams(vmem_limit_bytes=32 * 2**20),
        name="features",
    )(slab, far, core, w1, w2, wr, part, weights, blends, inner, ready)


def slots_kernel(by_lane_ref, one_hot):
    lo_iota = lax.broadcasted_iota(jnp.int32, (256, 1024), 0)
    for s in range(4):
        hit = lo_iota == (by_lane_ref[s : s + 1] >> 2)
        one_hot[:, 1024 * s : 1024 * s + 1024] = jnp.where(hit, 1.0, 0.0).astype(BF16)


def slots(by_lane):
    return pl.pallas_call(
        slots_kernel,
        out_shape=jax.ShapeDtypeStruct((256, 4096), BF16),
        in_specs=[whole(pltpu.VMEM)],
        out_specs=whole(pltpu.VMEM),
        compiler_params=pltpu.CompilerParams(vmem_limit_bytes=16 * 2**20),
        cost_estimate=pl.CostEstimate(flops=10**7, bytes_accessed=2 * 10**6, transcendentals=0),
        name="slots",
    )(by_lane)


def spread_kernel(pos_ref, val_ref, one_hot, by_row_ref, spread, facing):
    start = pl.multiple_of((pos_ref[0] % 2) * 96, 32)
    val = val_ref[...]
    hi_iota = lax.broadcasted_iota(jnp.int32, (1024, 128), 1) // 32
    sel_row = lax.broadcasted_iota(jnp.int32, (128, 128), 0)
    sel_col = lax.broadcasted_iota(jnp.int32, (128, 128), 1) % 32
    for s in range(4):
        select = jnp.where(sel_row == sel_col + 32 * s, 1.0, 0.0).astype(BF16)
        block = hi_iota == (by_row_ref[:, s : s + 1] & 3)
        spread[1024 * s : 1024 * s + 1024] = jnp.where(block, dot(val, select), 0.0).astype(BF16)
    for i in range(2):
        rows = one_hot[pl.ds(128 * i + start, 32), :]
        facing[i] = dot(rows, spread[...]).astype(BF16)


def spread_values(slab, val, one_hot, by_row):
    return pl.pallas_call(
        spread_kernel,
        out_shape=(
            jax.ShapeDtypeStruct((4096, 128), BF16),
            jax.ShapeDtypeStruct((2, 32, 128), BF16),
        ),
        in_specs=[whole(pltpu.SMEM)] + [whole(pltpu.VMEM)] * 3,
        out_specs=(whole(pltpu.VMEM),) * 2,
        compiler_params=pltpu.CompilerParams(vmem_limit_bytes=16 * 2**20),
        name="spread",
    )(slab, val, one_hot, by_row)


def scatter_kernel(one_hot, spread, out_ref):
    out_ref[...] = dot(one_hot[...], spread[...]).reshape(2, 128, 128).astype(BF16)


def scatter(one_hot, spread):
    return pl.pallas_call(
        scatter_kernel,
        out_shape=jax.ShapeDtypeStruct((2, 128, 128), BF16),
        in_specs=[whole(pltpu.VMEM)] * 2,
        out_specs=whole(pltpu.VMEM),
        compiler_params=pltpu.CompilerParams(vmem_limit_bytes=16 * 2**20),
        cost_estimate=pl.CostEstimate(flops=3 * 10**8, bytes_accessed=3 * 10**6, transcendentals=0),
        name="scatter",
    )(one_hot, spread)


def put_depth(dst, plane, x):
    step = lax.broadcasted_iota(jnp.int32, x.shape, 0) % 16
    lane = lax.broadcasted_iota(jnp.int32, x.shape, 1)
    rows = x.shape[0]
    before = jnp.where(step == 0, 0.0, pltpu.roll(x, 1, 0))
    after = jnp.where(step == 15, 0.0, pltpu.roll(x, rows - 1, 0))
    side = pltpu.roll(jnp.where(lane >= 96, before, after), 32, 1)
    dst[plane, :, 0:128] = x.astype(BF16)
    dst[plane, :, 128:256] = jnp.where(lane < 64, side, 0.0).astype(BF16)


def volume_start_kernel(own_ref, w_ref, acc, x1):
    for i in range(2):
        put_depth(x1, i, own_ref[i].astype(F32))
    zero = jnp.zeros((160, 128), F32)
    acc[0:160] = zero
    acc[480:640] = zero
    for k, dx in enumerate((1, 0, 2)):
        total = None
        for dy in range(3):
            rows = x1[:, dy * 16 : dy * 16 + 160, :].reshape(320, 256)
            part = dot_nt(rows, w_ref[dx * 3 + dy])
            total = part if total is None else total + part
        at = (2 - dx) * 160
        if k == 0:
            acc[at : at + 320] = total
        else:
            acc[at : at + 320] += total


def volume_start(own, w1):
    return pl.pallas_call(
        volume_start_kernel,
        out_shape=jax.ShapeDtypeStruct((640, 128), F32),
        in_specs=[whole(pltpu.VMEM)] * 2,
        out_specs=whole(pltpu.VMEM),
        scratch_shapes=[pltpu.VMEM((2, 192, 256), BF16)],
        compiler_params=pltpu.CompilerParams(vmem_limit_bytes=16 * 2**20),
        name="volume_start",
    )(own, w1)


def volume_kernel(
    pos_ref, own_ref, next_ref, near_ref, part_ref, w1_ref, w2_ref, out_ref, x1, x2, acc, packed
):
    p = pos_ref[0]
    q = pos_ref[1]
    even = (1 - p % 2).astype(F32)
    odd = 1.0 - even
    for i in range(2):
        near = near_ref[i].astype(F32)
        nxt = next_ref[i].astype(F32)
        put_depth(x1, i, even * nxt + odd * near)
        put_depth(x1, 2 + i, even * near + odd * nxt)
    sums = [part_ref[i * 160 : (i + 1) * 160] for i in range(4)]
    for dy in range(3):
        rows = slice(dy * 16, dy * 16 + 160)
        low0 = dot_nt(x1[0:2, rows, :].reshape(320, 256), w1_ref[dy])
        low1 = dot_nt(x1[1, rows, :], w1_ref[3 + dy])
        high1 = dot_nt(x1[2, rows, :], w1_ref[3 + dy])
        high2 = dot_nt(x1[2:4, rows, :].reshape(320, 256), w1_ref[6 + dy])
        sums[0] = sums[0] + low0[0:160] + low1
        sums[1] = sums[1] + low0[160:320]
        sums[2] = sums[2] + high2[0:160]
        sums[3] = sums[3] + high2[160:320] + high1
    y = lax.broadcasted_iota(jnp.int32, (160, 128), 0) // 16
    first_y = jnp.where(q == 0, 1, 0)
    last_y = jnp.where(q == 3, 8, 9)
    inside = (y >= first_y) & (y <= last_y)
    for i in range(4):
        h = jnp.where(inside, jnp.maximum(sums[i], 0.0), 0.0)
        if i == 0:
            h = h * jnp.where(p == 0, 0.0, 1.0)
        if i == 3:
            h = h * jnp.where(p == 31, 0.0, 1.0)
        put_depth(x2, i, h)
    for t in range(9):
        dx, dy = divmod(t, 3)
        part = dot_nt(x2[dx : dx + 2, dy * 16 : dy * 16 + 128, :].reshape(256, 256), w2_ref[t])
        if t == 0:
            acc[...] = part
        else:
            acc[...] += part
    for i in range(2):
        res = acc[i * 128 : (i + 1) * 128] + own_ref[i, 32:160].astype(F32)
        res = res.T
        for k in range(4):
            block = [res[32 * z : 32 * z + 32, 32 * k : 32 * k + 32] for z in range(4)]
            packed[pl.ds(2 * k + i, 32, stride=8), :] = jnp.concatenate(block, axis=1)
    source = lax.broadcasted_iota(jnp.int32, (128, 128), 0)
    target = lax.broadcasted_iota(jnp.int32, (128, 128), 1)
    place = jnp.where(target == (source % 32) * 4 + source // 32, 1.0, 0.0).astype(BF16)
    out_ref[...] = dot(packed[...].astype(BF16), place).astype(BF16)


def volume_convs(pos, own, nxt, near, part, w1, w2):
    return pl.pallas_call(
        volume_kernel,
        out_shape=jax.ShapeDtypeStruct((256, 128), BF16),
        in_specs=[whole(pltpu.SMEM)] + [whole(pltpu.VMEM)] * 6,
        out_specs=whole(pltpu.VMEM),
        scratch_shapes=[
            pltpu.VMEM((4, 192, 256), BF16),
            pltpu.VMEM((4, 160, 256), BF16),
            pltpu.VMEM((256, 128), F32),
            pltpu.VMEM((256, 128), F32),
        ],
        compiler_params=pltpu.CompilerParams(vmem_limit_bytes=32 * 2**20),
        name="volume",
    )(pos, own, nxt, near, part, w1, w2)


def banded(weight):
    taps = weight.reshape(9, 3, 32, 32)
    zero = jnp.zeros((9, 32, 32), weight.dtype)
    rows = []
    for z in range(4):
        blocks = [zero] * 8
        for dz in range(3):
            at = z + dz - 1
            blocks[4 if at < 0 else 5 if at > 3 else at] = taps[:, dz]
        rows.append(jnp.concatenate(blocks, axis=2))
    return jnp.concatenate(rows, axis=1)


def swap(x, partner, cams, slabs):
    pairs = []
    for p in range(cams):
        for s in range(slabs):
            to = partner(p, s)
            if 0 <= to[0] < cams and 0 <= to[1] < slabs:
                pairs.append((p * slabs + s, to[0] * slabs + to[1]))
    return lax.ppermute(x, AXES, pairs)


def core_partner(p, s):
    return p, s ^ 1


def far_partner(p, s):
    return p, (s + 1 if s % 2 else s - 1)


def near_partner(p, s):
    return p ^ 1, s


def next_partner(p, s):
    return (p + 1 if p % 2 else p - 1), s


def local(
    image,
    w_first,
    w_second,
    w_reduce,
    cam_weight,
    sample_pixel,
    sample_frac,
    voxel_slot,
    wv_first,
    wv_second,
):
    cams = lax.axis_size("cam")
    slabs = lax.axis_size("slab")
    p = lax.axis_index("cam")
    s = lax.axis_index("slab")
    even = s % 2 == 0
    img = image[0]
    top, bottom = img[0:3], img[1:4]
    far = swap(jnp.where(even, top, bottom), far_partner, cams, slabs)
    core = swap(jnp.where(even, bottom, top), core_partner, cams, slabs)

    pix = sample_pixel[0].T
    frac = jnp.transpose(sample_frac[0], (0, 2, 1))
    w1 = w_first.reshape(3, 384, 128)
    w2 = w_second.reshape(3, 384, 128)
    by_row = voxel_slot[0].reshape(1024, 4)
    by_lane = by_row.T
    band1 = banded(wv_first)
    band2 = banded(wv_second)
    slab_pos = s.astype(jnp.int32).reshape(1)

    part, weights, blends = prepare(cam_weight, img, w1, pix, frac)
    inner, ready = middle(slab_pos, core, w1, w2, w_reduce.T, part)
    sent = features(
        slab_pos, far, core, w1, w2, w_reduce.T, part, weights, blends, inner, ready
    )
    got = lax.all_to_all(sent.reshape(128, 8, 128), AXES, 0, 0, tiled=True).reshape(1024, 128)
    one_hot = slots(by_lane)
    spread, facing = spread_values(slab_pos, got, one_hot, by_row)
    far = swap(facing, far_partner, cams, slabs)
    volume = scatter(one_hot, spread)

    pos = jnp.stack([p, s]).astype(jnp.int32)
    top, bottom = volume[:, 0:32], volume[:, 96:128]
    core = swap(jnp.where(even, bottom, top), core_partner, cams, slabs)
    above = jnp.where(even, far, core)
    below = jnp.where(even, core, far)
    own = jnp.concatenate([above, volume, below], axis=1)
    nxt = swap(own, next_partner, cams, slabs)
    near = swap(own, near_partner, cams, slabs)
    part = volume_start(own, band1)
    out = volume_convs(pos, own, nxt, near, part, band1, band2)
    return out.reshape(32, 4, 2, 128).transpose(0, 2, 1, 3).reshape(32, 2, 512)


def solution(mesh):
    placed = (
        P(("dp", "cam"), "slab", None, None),
        P(),
        P(),
        P(),
        P("cam"),
        P(("dp", "cam", "slab"), None, None),
        P(("dp", "cam", "slab"), None, None, None),
        P(("dp", "cam", "slab"), None, None),
        P(),
        P(),
    )
    return jax.shard_map(
        local, mesh=mesh, in_specs=placed, out_specs=P(None, ("dp", "cam"), "slab"), check_vma=False
    )
```

```python
import jax
import jax.numpy as jnp
from jax import lax
from jax.experimental import pallas as pl
from jax.experimental.pallas import tpu as pltpu
from jax.sharding import PartitionSpec as P

AXES = ("cam", "slab")
F32 = jnp.float32
BF16 = jnp.bfloat16


def dot(a, b):
    return jnp.dot(a, b, preferred_element_type=F32)


def dot_nt(a, b):
    return lax.dot_general(a, b, (((1,), (1,)), ((), ())), preferred_element_type=F32)


def whole(memory_space):
    return pl.BlockSpec(memory_space=memory_space)


def put_columns(dst, row, x):
    cols = x.shape[0]
    pos = lax.broadcasted_iota(jnp.int32, x.shape, 0)
    left = jnp.where(pos == 0, 0.0, pltpu.roll(x, 1, 0))
    right = jnp.where(pos == cols - 1, 0.0, pltpu.roll(x, cols - 1, 0))
    dst[row, :, 0:128] = left.astype(BF16)
    dst[row, :, 128:256] = x.astype(BF16)
    dst[row, :, 256:384] = right.astype(BF16)


def lanes(x):
    return jnp.concatenate([x[i : i + 1] for i in range(4)], axis=1)


def sample_weights(scale_ref, pix_ref, frac_ref, weights, blends):
    scale = scale_ref[0]
    col_iota = lax.broadcasted_iota(jnp.int32, (256, 512), 0)
    row_iota = lax.broadcasted_iota(jnp.int32, (8, 512), 0)
    for k in range(8):
        pix = lanes(pix_ref[4 * k : 4 * k + 4])
        fr = lanes(frac_ref[0, 4 * k : 4 * k + 4])
        fc = lanes(frac_ref[1, 4 * k : 4 * k + 4])
        col = pix & 255
        row = pix >> 8
        weights[k] = jnp.where(
            col_iota == col, 1.0 - fc, jnp.where(col_iota == col + 1, fc, 0.0)
        ).astype(BF16)
        blends[k] = scale * jnp.where(
            row_iota == row, 1.0 - fr, jnp.where(row_iota == row + 1, fr, 0.0)
        )


def prepare_kernel(
    scale_ref, img_hbm, w1_hbm, pix_hbm, frac_hbm, acc, weights, blends,
    x1, img_ref, w1_ref, pix_ref, frac_ref, sems,
):
    pairs = ((pix_hbm, pix_ref), (frac_hbm, frac_ref), (img_hbm, img_ref), (w1_hbm, w1_ref))
    copies = [pltpu.make_async_copy(src, dst, sems.at[i]) for i, (src, dst) in enumerate(pairs)]
    for copy in copies:
        copy.start()
    copies[0].wait()
    copies[1].wait()
    sample_weights(scale_ref, pix_ref, frac_ref, weights, blends)
    copies[2].wait()
    copies[3].wait()
    for i in range(4):
        put_columns(x1, i, img_ref[i].astype(F32))
    own = x1[...].reshape(1024, 384)
    acc[0:512] = jnp.zeros((512, 128), F32)
    acc[1536:1792] = jnp.zeros((256, 128), F32)
    acc[512:1536] = dot(own, w1_ref[0])
    acc[256:1280] += dot(own, w1_ref[1])
    acc[0:1024] += dot(own, w1_ref[2])


def prepare(scale, img, w1, pix, frac):
    return pl.pallas_call(
        prepare_kernel,
        out_shape=(
            jax.ShapeDtypeStruct((1792, 128), F32),
            jax.ShapeDtypeStruct((8, 256, 512), BF16),
            jax.ShapeDtypeStruct((8, 8, 512), F32),
        ),
        in_specs=[whole(pltpu.SMEM)] + [whole(pltpu.HBM)] * 4,
        out_specs=(whole(pltpu.VMEM),) * 3,
        scratch_shapes=[
            pltpu.VMEM((4, 256, 384), BF16),
            pltpu.VMEM((4, 256, 128), BF16),
            pltpu.VMEM((3, 384, 128), BF16),
            pltpu.VMEM((32, 128), jnp.int32),
            pltpu.VMEM((2, 32, 128), F32),
            pltpu.SemaphoreType.DMA((4,)),
        ],
        compiler_params=pltpu.CompilerParams(vmem_limit_bytes=24 * 2**20),
        cost_estimate=pl.CostEstimate(flops=10000000000, bytes_accessed=4 * 10**6, transcendentals=0),
        name="prepare",
    )(scale, *(pltpu.with_memory_space_constraint(x, pltpu.HBM) for x in (img, w1, pix, frac)))


def table_rows(acc, at, count, wr):
    rows = []
    for i in range(at, at + count):
        h = jnp.maximum(acc[i * 256 : (i + 1) * 256], 0.0)
        rows.append(dot_nt(wr, h.astype(BF16)))
    return rows


def middle_kernel(pos_ref, core_ref, w1_ref, w2_ref, wr_ref, part_ref, inner, table, x1, x2, acc):
    @pl.when(pos_ref[0] % 2 == 0)
    def _():
        for i in range(3):
            put_columns(x1, i, core_ref[i].astype(F32))
        tail0 = dot(x1[0], w1_ref[0])
        tail1 = dot(x1[0:2].reshape(512, 384), w1_ref[1])
        tail2 = dot(x1[0:3].reshape(768, 384), w1_ref[2])
        for i in range(2, 7):
            h = part_ref[i * 256 : (i + 1) * 256]
            if i == 4:
                h = h + tail2[0:256]
            elif i == 5:
                h = h + tail2[256:512] + tail1[0:256]
            elif i == 6:
                h = h + tail2[512:768] + tail1[256:512] + tail0
            put_columns(x2, i - 2, jnp.maximum(h, 0.0))
        inner[...] = x2[0:2]
        acc[...] = dot(x2[0:3].reshape(768, 384), w2_ref[0])
        acc[...] += dot(x2[1:4].reshape(768, 384), w2_ref[1])
        acc[...] += dot(x2[2:5].reshape(768, 384), w2_ref[2])
        table[...] = jnp.concatenate(table_rows(acc, 0, 3, wr_ref[...]), axis=0).astype(BF16)


def middle(slab, core, w1, w2, wr, part):
    return pl.pallas_call(
        middle_kernel,
        out_shape=(
            jax.ShapeDtypeStruct((2, 256, 384), BF16),
            jax.ShapeDtypeStruct((96, 256), BF16),
        ),
        in_specs=[whole(pltpu.SMEM)] + [whole(pltpu.VMEM)] * 5,
        out_specs=(whole(pltpu.VMEM),) * 2,
        scratch_shapes=[
            pltpu.VMEM((3, 256, 384), BF16),
            pltpu.VMEM((5, 256, 384), BF16),
            pltpu.VMEM((768, 128), F32),
        ],
        compiler_params=pltpu.CompilerParams(vmem_limit_bytes=24 * 2**20),
        cost_estimate=pl.CostEstimate(flops=1000000, bytes_accessed=10**3, transcendentals=0),
        name="middle",
    )(slab, core, w1, w2, wr, part)


def features_kernel(
    pos_ref, far_ref, core_ref, w1_ref, w2_ref, wr_ref, part_ref, weights, blends,
    inner, ready, out_ref, x1, x2, acc, table, packed,
):
    slab = pos_ref[0]
    not_first = jnp.where(slab == 0, 0.0, 1.0)
    not_last = jnp.where(slab == 3, 0.0, 1.0)

    def first_rows(above):
        for i in range(2):
            put_columns(x1, i, above[1 + i].astype(F32))
        head = dot(x1[0:2].reshape(512, 384), w1_ref[0])
        return head[0:256] + dot(x1[1], w1_ref[1]), head[256:512]

    @pl.when(slab % 2 == 0)
    def _():
        head0, head1 = first_rows(far_ref)
        put_columns(x2, 0, jnp.maximum(part_ref[0:256] + head0, 0.0) * not_first)
        put_columns(x2, 1, jnp.maximum(part_ref[256:512] + head1, 0.0))
        x2[2:4] = inner[...]
        acc[0:512] = dot(x2[0:2].reshape(512, 384), w2_ref[0])
        acc[0:512] += dot(x2[1:3].reshape(512, 384), w2_ref[1])
        acc[0:512] += dot(x2[2:4].reshape(512, 384), w2_ref[2])
        table[0:64] = jnp.concatenate(table_rows(acc, 0, 2, wr_ref[...]), axis=0).astype(BF16)
        table[64:160] = ready[...]

    @pl.when(slab % 2 == 1)
    def _():
        head0, head1 = first_rows(core_ref)
        for i in range(3):
            put_columns(x1, 2 + i, far_ref[i].astype(F32))
        tail0 = dot(x1[2], w1_ref[0])
        tail1 = dot(x1[2:4].reshape(512, 384), w1_ref[1])
        tail2 = dot(x1[2:5].reshape(768, 384), w1_ref[2])
        for i in range(7):
            h = part_ref[i * 256 : (i + 1) * 256]
            if i == 0:
                h = h + head0
            elif i == 1:
                h = h + head1
            elif i == 4:
                h = h + tail2[0:256]
            elif i == 5:
                h = h + tail2[256:512] + tail1[0:256]
            elif i == 6:
                h = h + tail2[512:768] + tail1[256:512] + tail0
            h = jnp.maximum(h, 0.0)
            if i >= 5:
                h = h * not_last
            put_columns(x2, i, h)
        acc[...] = dot(x2[0:5].reshape(1280, 384), w2_ref[0])
        acc[...] += dot(x2[1:6].reshape(1280, 384), w2_ref[1])
        acc[...] += dot(x2[2:7].reshape(1280, 384), w2_ref[2])
        rows = table_rows(acc, 0, 5, wr_ref[...])
        rows[4] = rows[4] * not_last
        table[...] = jnp.concatenate(rows, axis=0).astype(BF16)

    for k in range(8):
        got = dot(table[...], weights[k])
        blend = blends[k]
        total = got[0:32] * blend[0:1]
        for r in range(1, 5):
            total = total + got[32 * r : 32 * r + 32] * blend[r : r + 1]
        block = jnp.concatenate([total[:, 128 * i : 128 * i + 128] for i in range(4)], axis=0)
        packed[pl.ds(k, 128, stride=8), :] = block.T
    out_ref[...] = packed[...].astype(BF16)


def features(slab, far, core, w1, w2, wr, part, weights, blends, inner, ready):
    return pl.pallas_call(
        features_kernel,
        out_shape=jax.ShapeDtypeStruct((1024, 128), BF16),
        in_specs=[whole(pltpu.SMEM)] + [whole(pltpu.VMEM)] * 10,
        out_specs=whole(pltpu.VMEM),
        scratch_shapes=[
            pltpu.VMEM((5, 256, 384), BF16),
            pltpu.VMEM((7, 256, 384), BF16),
            pltpu.VMEM((1280, 128), F32),
            pltpu.VMEM((160, 256), BF16),
            pltpu.VMEM((1024, 128), F32),
        ],
        compiler_params=pltpu.CompilerParams(vmem_limit_bytes=32 * 2**20),
        name="features",
    )(slab, far, core, w1, w2, wr, part, weights, blends, inner, ready)


def slots_kernel(pos_ref, by_lane_ref, one_hot):
    row = lax.broadcasted_iota(jnp.int32, (256, 1024), 0)
    start = (pos_ref[0] % 2) * 96
    voxel = (row // 32 % 2 * 128 + start + row % 32) * 4 + row // 64
    for s in range(4):
        hit = voxel == by_lane_ref[s : s + 1]
        one_hot[:, 1024 * s : 1024 * s + 1024] = jnp.where(hit, 1.0, 0.0).astype(BF16)


def slots(slab, by_lane):
    return pl.pallas_call(
        slots_kernel,
        out_shape=jax.ShapeDtypeStruct((256, 4096), BF16),
        in_specs=[whole(pltpu.SMEM), whole(pltpu.VMEM)],
        out_specs=whole(pltpu.VMEM),
        compiler_params=pltpu.CompilerParams(vmem_limit_bytes=16 * 2**20),
        cost_estimate=pl.CostEstimate(flops=10**7, bytes_accessed=2 * 10**6, transcendentals=0),
        name="slots",
    )(slab, by_lane)


def facing_kernel(val_ref, one_hot, out_ref):
    group = lax.broadcasted_iota(jnp.int32, (256, 128), 1) // 32
    val = val_ref[...]
    total = jnp.zeros((256, 128), F32)
    for s in range(4):
        part = dot(one_hot[:, 1024 * s : 1024 * s + 1024], val)
        total = jnp.where(group == s, part, total)
    total = total + pltpu.roll(total, 64, 1)
    total = total + pltpu.roll(total, 32, 1)
    group = group[0:64]
    rows = jnp.zeros((64, 128), F32)
    for z in range(4):
        rows = jnp.where(group == z, total[64 * z : 64 * z + 64], rows)
    out_ref[...] = rows.reshape(2, 32, 128).astype(BF16)


def facing_rows(val, one_hot):
    return pl.pallas_call(
        facing_kernel,
        out_shape=jax.ShapeDtypeStruct((2, 32, 128), BF16),
        in_specs=[whole(pltpu.VMEM)] * 2,
        out_specs=whole(pltpu.VMEM),
        compiler_params=pltpu.CompilerParams(vmem_limit_bytes=16 * 2**20),
        name="facing",
    )(val, one_hot)


def scatter_kernel(val_ref, by_lane_ref, by_row_ref, out_ref):
    val = val_ref[...]
    lo_iota = lax.broadcasted_iota(jnp.int32, (256, 1024), 0)
    hi_iota = lax.broadcasted_iota(jnp.int32, (1024, 128), 1) // 32
    sel_row = lax.broadcasted_iota(jnp.int32, (128, 128), 0)
    sel_col = lax.broadcasted_iota(jnp.int32, (128, 128), 1) % 32
    total = jnp.zeros((256, 128), F32)
    for s in range(4):
        one_hot = jnp.where(lo_iota == (by_lane_ref[s : s + 1] >> 2), 1.0, 0.0).astype(BF16)
        select = jnp.where(sel_row == sel_col + 32 * s, 1.0, 0.0).astype(BF16)
        spread = dot(val, select)
        hi = by_row_ref[:, s : s + 1] & 3
        spread = jnp.where(hi_iota == hi, spread, 0.0).astype(BF16)
        total = total + dot(one_hot, spread)
    out_ref[...] = total.reshape(2, 128, 128).astype(BF16)


def scatter(val, by_lane, by_row):
    return pl.pallas_call(
        scatter_kernel,
        out_shape=jax.ShapeDtypeStruct((2, 128, 128), BF16),
        in_specs=[whole(pltpu.VMEM)] * 3,
        out_specs=whole(pltpu.VMEM),
        compiler_params=pltpu.CompilerParams(vmem_limit_bytes=16 * 2**20),
        cost_estimate=pl.CostEstimate(flops=3 * 10**8, bytes_accessed=3 * 10**6, transcendentals=0),
        name="scatter",
    )(val, by_lane, by_row)


def put_depth(dst, plane, x):
    step = lax.broadcasted_iota(jnp.int32, x.shape, 0) % 16
    lane = lax.broadcasted_iota(jnp.int32, x.shape, 1)
    rows = x.shape[0]
    before = jnp.where(step == 0, 0.0, pltpu.roll(x, 1, 0))
    after = jnp.where(step == 15, 0.0, pltpu.roll(x, rows - 1, 0))
    side = pltpu.roll(jnp.where(lane >= 96, before, after), 32, 1)
    dst[plane, :, 0:128] = x.astype(BF16)
    dst[plane, :, 128:256] = jnp.where(lane < 64, side, 0.0).astype(BF16)


def volume_start_kernel(own_ref, w_ref, acc, x1):
    for i in range(2):
        put_depth(x1, i, own_ref[i].astype(F32))
    zero = jnp.zeros((160, 128), F32)
    acc[0:160] = zero
    acc[480:640] = zero
    for k, dx in enumerate((1, 0, 2)):
        total = None
        for dy in range(3):
            rows = x1[:, dy * 16 : dy * 16 + 160, :].reshape(320, 256)
            part = dot_nt(rows, w_ref[dx * 3 + dy])
            total = part if total is None else total + part
        at = (2 - dx) * 160
        if k == 0:
            acc[at : at + 320] = total
        else:
            acc[at : at + 320] += total


def volume_start(own, w1):
    return pl.pallas_call(
        volume_start_kernel,
        out_shape=jax.ShapeDtypeStruct((640, 128), F32),
        in_specs=[whole(pltpu.VMEM)] * 2,
        out_specs=whole(pltpu.VMEM),
        scratch_shapes=[pltpu.VMEM((2, 192, 256), BF16)],
        compiler_params=pltpu.CompilerParams(vmem_limit_bytes=16 * 2**20),
        name="volume_start",
    )(own, w1)


def volume_kernel(
    pos_ref, own_ref, next_ref, near_ref, part_ref, w1_ref, w2_ref, out_ref, x1, x2, acc, packed
):
    p = pos_ref[0]
    q = pos_ref[1]
    even = (1 - p % 2).astype(F32)
    odd = 1.0 - even
    for i in range(2):
        near = near_ref[i].astype(F32)
        nxt = next_ref[i].astype(F32)
        put_depth(x1, i, even * nxt + odd * near)
        put_depth(x1, 2 + i, even * near + odd * nxt)
    sums = [part_ref[i * 160 : (i + 1) * 160] for i in range(4)]
    for dy in range(3):
        rows = slice(dy * 16, dy * 16 + 160)
        low0 = dot_nt(x1[0:2, rows, :].reshape(320, 256), w1_ref[dy])
        low1 = dot_nt(x1[1, rows, :], w1_ref[3 + dy])
        high1 = dot_nt(x1[2, rows, :], w1_ref[3 + dy])
        high2 = dot_nt(x1[2:4, rows, :].reshape(320, 256), w1_ref[6 + dy])
        sums[0] = sums[0] + low0[0:160] + low1
        sums[1] = sums[1] + low0[160:320]
        sums[2] = sums[2] + high2[0:160]
        sums[3] = sums[3] + high2[160:320] + high1
    y = lax.broadcasted_iota(jnp.int32, (160, 128), 0) // 16
    first_y = jnp.where(q == 0, 1, 0)
    last_y = jnp.where(q == 3, 8, 9)
    inside = (y >= first_y) & (y <= last_y)
    for i in range(4):
        h = jnp.where(inside, jnp.maximum(sums[i], 0.0), 0.0)
        if i == 0:
            h = h * jnp.where(p == 0, 0.0, 1.0)
        if i == 3:
            h = h * jnp.where(p == 31, 0.0, 1.0)
        put_depth(x2, i, h)
    for t in range(9):
        dx, dy = divmod(t, 3)
        part = dot_nt(x2[dx : dx + 2, dy * 16 : dy * 16 + 128, :].reshape(256, 256), w2_ref[t])
        if t == 0:
            acc[...] = part
        else:
            acc[...] += part
    for i in range(2):
        res = acc[i * 128 : (i + 1) * 128] + own_ref[i, 32:160].astype(F32)
        res = res.T
        for k in range(4):
            block = [res[32 * z : 32 * z + 32, 32 * k : 32 * k + 32] for z in range(4)]
            packed[pl.ds(2 * k + i, 32, stride=8), :] = jnp.concatenate(block, axis=1)
    source = lax.broadcasted_iota(jnp.int32, (128, 128), 0)
    target = lax.broadcasted_iota(jnp.int32, (128, 128), 1)
    place = jnp.where(target == (source % 32) * 4 + source // 32, 1.0, 0.0).astype(BF16)
    out_ref[...] = dot(packed[...].astype(BF16), place).astype(BF16)


def volume_convs(pos, own, nxt, near, part, w1, w2):
    return pl.pallas_call(
        volume_kernel,
        out_shape=jax.ShapeDtypeStruct((256, 128), BF16),
        in_specs=[whole(pltpu.SMEM)] + [whole(pltpu.VMEM)] * 6,
        out_specs=whole(pltpu.VMEM),
        scratch_shapes=[
            pltpu.VMEM((4, 192, 256), BF16),
            pltpu.VMEM((4, 160, 256), BF16),
            pltpu.VMEM((256, 128), F32),
            pltpu.VMEM((256, 128), F32),
        ],
        compiler_params=pltpu.CompilerParams(vmem_limit_bytes=32 * 2**20),
        name="volume",
    )(pos, own, nxt, near, part, w1, w2)


def banded(weight):
    taps = weight.reshape(9, 3, 32, 32)
    zero = jnp.zeros((9, 32, 32), weight.dtype)
    rows = []
    for z in range(4):
        blocks = [zero] * 8
        for dz in range(3):
            at = z + dz - 1
            blocks[4 if at < 0 else 5 if at > 3 else at] = taps[:, dz]
        rows.append(jnp.concatenate(blocks, axis=2))
    return jnp.concatenate(rows, axis=1)


def swap(x, partner, cams, slabs):
    pairs = []
    for p in range(cams):
        for s in range(slabs):
            to = partner(p, s)
            if 0 <= to[0] < cams and 0 <= to[1] < slabs:
                pairs.append((p * slabs + s, to[0] * slabs + to[1]))
    return lax.ppermute(x, AXES, pairs)


def core_partner(p, s):
    return p, s ^ 1


def far_partner(p, s):
    return p, (s + 1 if s % 2 else s - 1)


def near_partner(p, s):
    return p ^ 1, s


def next_partner(p, s):
    return (p + 1 if p % 2 else p - 1), s


def local(
    image,
    w_first,
    w_second,
    w_reduce,
    cam_weight,
    sample_pixel,
    sample_frac,
    voxel_slot,
    wv_first,
    wv_second,
):
    cams = lax.axis_size("cam")
    slabs = lax.axis_size("slab")
    p = lax.axis_index("cam")
    s = lax.axis_index("slab")
    even = s % 2 == 0
    img = image[0]
    top, bottom = img[0:3], img[1:4]
    far = swap(jnp.where(even, top, bottom), far_partner, cams, slabs)
    core = swap(jnp.where(even, bottom, top), core_partner, cams, slabs)

    pix = sample_pixel[0].T
    frac = jnp.transpose(sample_frac[0], (0, 2, 1))
    w1 = w_first.reshape(3, 384, 128)
    w2 = w_second.reshape(3, 384, 128)
    by_row = voxel_slot[0].reshape(1024, 4)
    by_lane = by_row.T
    band1 = banded(wv_first)
    band2 = banded(wv_second)
    slab_pos = s.astype(jnp.int32).reshape(1)

    part, weights, blends = prepare(cam_weight, img, w1, pix, frac)
    inner, ready = middle(slab_pos, core, w1, w2, w_reduce.T, part)
    sent = features(
        slab_pos, far, core, w1, w2, w_reduce.T, part, weights, blends, inner, ready
    )
    got = lax.all_to_all(sent.reshape(128, 8, 128), AXES, 0, 0, tiled=True).reshape(1024, 128)
    facing = facing_rows(got, slots(slab_pos, by_lane))
    facing, got = lax.optimization_barrier((facing, got))
    far = swap(facing, far_partner, cams, slabs)
    volume = scatter(got, by_lane, by_row)

    pos = jnp.stack([p, s]).astype(jnp.int32)
    top, bottom = volume[:, 0:32], volume[:, 96:128]
    core = swap(jnp.where(even, bottom, top), core_partner, cams, slabs)
    above = jnp.where(even, far, core)
    below = jnp.where(even, core, far)
    own = jnp.concatenate([above, volume, below], axis=1)
    nxt = swap(own, next_partner, cams, slabs)
    near = swap(own, near_partner, cams, slabs)
    part = volume_start(own, band1)
    out = volume_convs(pos, own, nxt, near, part, band1, band2)
    return out.reshape(32, 4, 2, 128).transpose(0, 2, 1, 3).reshape(32, 2, 512)


def solution(mesh):
    placed = (
        P(("dp", "cam"), "slab", None, None),
        P(),
        P(),
        P(),
        P("cam"),
        P(("dp", "cam", "slab"), None, None),
        P(("dp", "cam", "slab"), None, None, None),
        P(("dp", "cam", "slab"), None, None),
        P(),
        P(),
    )
    return jax.shard_map(
        local, mesh=mesh, in_specs=placed, out_specs=P(None, ("dp", "cam"), "slab"), check_vma=False
    )
```

```python
import jax
import jax.numpy as jnp
from jax import lax
from jax.experimental import pallas as pl
from jax.experimental.pallas import tpu as pltpu
from jax.sharding import PartitionSpec as P

AXES = ("cam", "slab")
F32 = jnp.float32
BF16 = jnp.bfloat16


def dot(a, b):
    return jnp.dot(a, b, preferred_element_type=F32)


def dot_nt(a, b):
    return lax.dot_general(a, b, (((1,), (1,)), ((), ())), preferred_element_type=F32)


def whole(memory_space):
    return pl.BlockSpec(memory_space=memory_space)


def put_columns(dst, row, x):
    cols = x.shape[0]
    pos = lax.broadcasted_iota(jnp.int32, x.shape, 0)
    left = jnp.where(pos == 0, 0.0, pltpu.roll(x, 1, 0))
    right = jnp.where(pos == cols - 1, 0.0, pltpu.roll(x, cols - 1, 0))
    dst[row, :, 0:128] = left.astype(BF16)
    dst[row, :, 128:256] = x.astype(BF16)
    dst[row, :, 256:384] = right.astype(BF16)


def lanes(x):
    return jnp.concatenate([x[i : i + 1] for i in range(4)], axis=1)


def sample_weights(scale_ref, pix_ref, frac_ref, weights, blends):
    scale = scale_ref[0]
    col_iota = lax.broadcasted_iota(jnp.int32, (256, 512), 0)
    row_iota = lax.broadcasted_iota(jnp.int32, (8, 512), 0)
    for k in range(8):
        pix = lanes(pix_ref[4 * k : 4 * k + 4])
        fr = lanes(frac_ref[0, 4 * k : 4 * k + 4])
        fc = lanes(frac_ref[1, 4 * k : 4 * k + 4])
        col = pix & 255
        row = pix >> 8
        weights[k] = jnp.where(
            col_iota == col, 1.0 - fc, jnp.where(col_iota == col + 1, fc, 0.0)
        ).astype(BF16)
        blends[k] = scale * jnp.where(
            row_iota == row, 1.0 - fr, jnp.where(row_iota == row + 1, fr, 0.0)
        )


def prepare_kernel(
    scale_ref, img_hbm, w1_hbm, pix_hbm, frac_hbm, acc, weights, blends,
    x1, img_ref, w1_ref, pix_ref, frac_ref, sems,
):
    pairs = ((pix_hbm, pix_ref), (frac_hbm, frac_ref), (img_hbm, img_ref), (w1_hbm, w1_ref))
    copies = [pltpu.make_async_copy(src, dst, sems.at[i]) for i, (src, dst) in enumerate(pairs)]
    for copy in copies:
        copy.start()
    copies[0].wait()
    copies[1].wait()
    sample_weights(scale_ref, pix_ref, frac_ref, weights, blends)
    copies[2].wait()
    copies[3].wait()
    for i in range(4):
        put_columns(x1, i, img_ref[i].astype(F32))
    own = x1[...].reshape(1024, 384)
    acc[0:512] = jnp.zeros((512, 128), F32)
    acc[1536:1792] = jnp.zeros((256, 128), F32)
    acc[512:1536] = dot(own, w1_ref[0])
    acc[256:1280] += dot(own, w1_ref[1])
    acc[0:1024] += dot(own, w1_ref[2])


def prepare(scale, img, w1, pix, frac):
    return pl.pallas_call(
        prepare_kernel,
        out_shape=(
            jax.ShapeDtypeStruct((1792, 128), F32),
            jax.ShapeDtypeStruct((8, 256, 512), BF16),
            jax.ShapeDtypeStruct((8, 8, 512), F32),
        ),
        in_specs=[whole(pltpu.SMEM)] + [whole(pltpu.HBM)] * 4,
        out_specs=(whole(pltpu.VMEM),) * 3,
        scratch_shapes=[
            pltpu.VMEM((4, 256, 384), BF16),
            pltpu.VMEM((4, 256, 128), BF16),
            pltpu.VMEM((3, 384, 128), BF16),
            pltpu.VMEM((32, 128), jnp.int32),
            pltpu.VMEM((2, 32, 128), F32),
            pltpu.SemaphoreType.DMA((4,)),
        ],
        compiler_params=pltpu.CompilerParams(vmem_limit_bytes=24 * 2**20),
        cost_estimate=pl.CostEstimate(flops=10000000000, bytes_accessed=4 * 10**6, transcendentals=0),
        name="prepare",
    )(scale, *(pltpu.with_memory_space_constraint(x, pltpu.HBM) for x in (img, w1, pix, frac)))


def table_rows(acc, at, count, wr):
    rows = []
    for i in range(at, at + count):
        h = jnp.maximum(acc[i * 256 : (i + 1) * 256], 0.0)
        rows.append(dot_nt(wr, h.astype(BF16)))
    return rows


def middle_kernel(pos_ref, core_ref, w1_ref, w2_ref, wr_ref, part_ref, inner, table, x1, x2, acc):
    @pl.when(pos_ref[0] % 2 == 0)
    def _():
        for i in range(3):
            put_columns(x1, i, core_ref[i].astype(F32))
        tail0 = dot(x1[0], w1_ref[0])
        tail1 = dot(x1[0:2].reshape(512, 384), w1_ref[1])
        tail2 = dot(x1[0:3].reshape(768, 384), w1_ref[2])
        for i in range(2, 7):
            h = part_ref[i * 256 : (i + 1) * 256]
            if i == 4:
                h = h + tail2[0:256]
            elif i == 5:
                h = h + tail2[256:512] + tail1[0:256]
            elif i == 6:
                h = h + tail2[512:768] + tail1[256:512] + tail0
            put_columns(x2, i - 2, jnp.maximum(h, 0.0))
        inner[...] = x2[0:2]
        acc[...] = dot(x2[0:3].reshape(768, 384), w2_ref[0])
        acc[...] += dot(x2[1:4].reshape(768, 384), w2_ref[1])
        acc[...] += dot(x2[2:5].reshape(768, 384), w2_ref[2])
        table[...] = jnp.concatenate(table_rows(acc, 0, 3, wr_ref[...]), axis=0).astype(BF16)


def middle(slab, core, w1, w2, wr, part):
    return pl.pallas_call(
        middle_kernel,
        out_shape=(
            jax.ShapeDtypeStruct((2, 256, 384), BF16),
            jax.ShapeDtypeStruct((96, 256), BF16),
        ),
        in_specs=[whole(pltpu.SMEM)] + [whole(pltpu.VMEM)] * 5,
        out_specs=(whole(pltpu.VMEM),) * 2,
        scratch_shapes=[
            pltpu.VMEM((3, 256, 384), BF16),
            pltpu.VMEM((5, 256, 384), BF16),
            pltpu.VMEM((768, 128), F32),
        ],
        compiler_params=pltpu.CompilerParams(vmem_limit_bytes=24 * 2**20),
        cost_estimate=pl.CostEstimate(flops=1000000, bytes_accessed=10**3, transcendentals=0),
        name="middle",
    )(slab, core, w1, w2, wr, part)


def features_kernel(
    pos_ref, far_ref, core_ref, w1_ref, w2_ref, wr_ref, part_ref, weights, blends,
    inner, ready, out_ref, x1, x2, acc, table, packed,
):
    slab = pos_ref[0]
    not_first = jnp.where(slab == 0, 0.0, 1.0)
    not_last = jnp.where(slab == 3, 0.0, 1.0)

    def first_rows(above):
        for i in range(2):
            put_columns(x1, i, above[1 + i].astype(F32))
        head = dot(x1[0:2].reshape(512, 384), w1_ref[0])
        return head[0:256] + dot(x1[1], w1_ref[1]), head[256:512]

    @pl.when(slab % 2 == 0)
    def _():
        head0, head1 = first_rows(far_ref)
        put_columns(x2, 0, jnp.maximum(part_ref[0:256] + head0, 0.0) * not_first)
        put_columns(x2, 1, jnp.maximum(part_ref[256:512] + head1, 0.0))
        x2[2:4] = inner[...]
        acc[0:512] = dot(x2[0:2].reshape(512, 384), w2_ref[0])
        acc[0:512] += dot(x2[1:3].reshape(512, 384), w2_ref[1])
        acc[0:512] += dot(x2[2:4].reshape(512, 384), w2_ref[2])
        table[0:64] = jnp.concatenate(table_rows(acc, 0, 2, wr_ref[...]), axis=0).astype(BF16)
        table[64:160] = ready[...]

    @pl.when(slab % 2 == 1)
    def _():
        head0, head1 = first_rows(core_ref)
        for i in range(3):
            put_columns(x1, 2 + i, far_ref[i].astype(F32))
        tail0 = dot(x1[2], w1_ref[0])
        tail1 = dot(x1[2:4].reshape(512, 384), w1_ref[1])
        tail2 = dot(x1[2:5].reshape(768, 384), w1_ref[2])
        for i in range(7):
            h = part_ref[i * 256 : (i + 1) * 256]
            if i == 0:
                h = h + head0
            elif i == 1:
                h = h + head1
            elif i == 4:
                h = h + tail2[0:256]
            elif i == 5:
                h = h + tail2[256:512] + tail1[0:256]
            elif i == 6:
                h = h + tail2[512:768] + tail1[256:512] + tail0
            h = jnp.maximum(h, 0.0)
            if i >= 5:
                h = h * not_last
            put_columns(x2, i, h)
        acc[...] = dot(x2[0:5].reshape(1280, 384), w2_ref[0])
        acc[...] += dot(x2[1:6].reshape(1280, 384), w2_ref[1])
        acc[...] += dot(x2[2:7].reshape(1280, 384), w2_ref[2])
        rows = table_rows(acc, 0, 5, wr_ref[...])
        rows[4] = rows[4] * not_last
        table[...] = jnp.concatenate(rows, axis=0).astype(BF16)

    for k in range(8):
        got = dot(table[...], weights[k])
        blend = blends[k]
        total = got[0:32] * blend[0:1]
        for r in range(1, 5):
            total = total + got[32 * r : 32 * r + 32] * blend[r : r + 1]
        block = jnp.concatenate([total[:, 128 * i : 128 * i + 128] for i in range(4)], axis=0)
        packed[pl.ds(k, 128, stride=8), :] = block.T
    out_ref[...] = packed[...].astype(BF16)


def features(slab, far, core, w1, w2, wr, part, weights, blends, inner, ready):
    return pl.pallas_call(
        features_kernel,
        out_shape=jax.ShapeDtypeStruct((1024, 128), BF16),
        in_specs=[whole(pltpu.SMEM)] + [whole(pltpu.VMEM)] * 10,
        out_specs=whole(pltpu.VMEM),
        scratch_shapes=[
            pltpu.VMEM((5, 256, 384), BF16),
            pltpu.VMEM((7, 256, 384), BF16),
            pltpu.VMEM((1280, 128), F32),
            pltpu.VMEM((160, 256), BF16),
            pltpu.VMEM((1024, 128), F32),
        ],
        compiler_params=pltpu.CompilerParams(vmem_limit_bytes=32 * 2**20),
        name="features",
    )(slab, far, core, w1, w2, wr, part, weights, blends, inner, ready)


def slots_kernel(pos_ref, by_lane_ref, one_hot):
    row = lax.broadcasted_iota(jnp.int32, (256, 1024), 0)
    start = (pos_ref[0] % 2) * 96
    voxel = (row // 32 % 2 * 128 + start + row % 32) * 4 + row // 64
    for s in range(4):
        hit = voxel == by_lane_ref[s : s + 1]
        one_hot[:, 1024 * s : 1024 * s + 1024] = jnp.where(hit, 1.0, 0.0).astype(BF16)


def slots(slab, by_lane):
    return pl.pallas_call(
        slots_kernel,
        out_shape=jax.ShapeDtypeStruct((256, 4096), BF16),
        in_specs=[whole(pltpu.SMEM), whole(pltpu.VMEM)],
        out_specs=whole(pltpu.VMEM),
        compiler_params=pltpu.CompilerParams(vmem_limit_bytes=16 * 2**20),
        cost_estimate=pl.CostEstimate(flops=10**7, bytes_accessed=2 * 10**6, transcendentals=0),
        name="slots",
    )(slab, by_lane)


def facing_kernel(val_ref, one_hot, out_ref):
    group = lax.broadcasted_iota(jnp.int32, (256, 128), 1) // 32
    val = val_ref[...]
    total = jnp.zeros((256, 128), F32)
    for s in range(4):
        part = dot(one_hot[:, 1024 * s : 1024 * s + 1024], val)
        total = jnp.where(group == s, part, total)
    total = total + pltpu.roll(total, 64, 1)
    total = total + pltpu.roll(total, 32, 1)
    group = group[0:64]
    rows = jnp.zeros((64, 128), F32)
    for z in range(4):
        rows = jnp.where(group == z, total[64 * z : 64 * z + 64], rows)
    out_ref[...] = rows.reshape(2, 32, 128).astype(BF16)


def facing_rows(val, one_hot):
    return pl.pallas_call(
        facing_kernel,
        out_shape=jax.ShapeDtypeStruct((2, 32, 128), BF16),
        in_specs=[whole(pltpu.VMEM)] * 2,
        out_specs=whole(pltpu.VMEM),
        compiler_params=pltpu.CompilerParams(vmem_limit_bytes=16 * 2**20),
        name="facing",
    )(val, one_hot)


def scatter_kernel(val_ref, by_lane_ref, by_row_ref, out_ref):
    val = val_ref[...]
    lo_iota = lax.broadcasted_iota(jnp.int32, (256, 1024), 0)
    hi_iota = lax.broadcasted_iota(jnp.int32, (1024, 128), 1) // 32
    sel_row = lax.broadcasted_iota(jnp.int32, (128, 128), 0)
    sel_col = lax.broadcasted_iota(jnp.int32, (128, 128), 1) % 32
    total = jnp.zeros((256, 128), F32)
    for s in range(4):
        one_hot = jnp.where(lo_iota == (by_lane_ref[s : s + 1] >> 2), 1.0, 0.0).astype(BF16)
        select = jnp.where(sel_row == sel_col + 32 * s, 1.0, 0.0).astype(BF16)
        spread = dot(val, select)
        hi = by_row_ref[:, s : s + 1] & 3
        spread = jnp.where(hi_iota == hi, spread, 0.0).astype(BF16)
        total = total + dot(one_hot, spread)
    out_ref[...] = total.reshape(2, 128, 128).astype(BF16)


def scatter(val, by_lane, by_row):
    return pl.pallas_call(
        scatter_kernel,
        out_shape=jax.ShapeDtypeStruct((2, 128, 128), BF16),
        in_specs=[whole(pltpu.VMEM)] * 3,
        out_specs=whole(pltpu.VMEM),
        compiler_params=pltpu.CompilerParams(vmem_limit_bytes=16 * 2**20),
        cost_estimate=pl.CostEstimate(flops=3 * 10**8, bytes_accessed=3 * 10**6, transcendentals=0),
        name="scatter",
    )(val, by_lane, by_row)


def put_depth(dst, plane, x):
    step = lax.broadcasted_iota(jnp.int32, x.shape, 0) % 16
    lane = lax.broadcasted_iota(jnp.int32, x.shape, 1)
    rows = x.shape[0]
    before = jnp.where(step == 0, 0.0, pltpu.roll(x, 1, 0))
    after = jnp.where(step == 15, 0.0, pltpu.roll(x, rows - 1, 0))
    side = pltpu.roll(jnp.where(lane >= 96, before, after), 32, 1)
    dst[plane, :, 0:128] = x.astype(BF16)
    dst[plane, :, 128:256] = jnp.where(lane < 64, side, 0.0).astype(BF16)


def volume_start_kernel(own_ref, w_ref, acc, x1):
    for i in range(2):
        put_depth(x1, i, own_ref[i].astype(F32))
    zero = jnp.zeros((160, 128), F32)
    acc[0:160] = zero
    acc[480:640] = zero
    for k, dx in enumerate((1, 0, 2)):
        total = None
        for dy in range(3):
            rows = x1[:, dy * 16 : dy * 16 + 160, :].reshape(320, 256)
            part = dot_nt(rows, w_ref[dx * 3 + dy])
            total = part if total is None else total + part
        at = (2 - dx) * 160
        if k == 0:
            acc[at : at + 320] = total
        else:
            acc[at : at + 320] += total


def volume_start(own, w1):
    return pl.pallas_call(
        volume_start_kernel,
        out_shape=jax.ShapeDtypeStruct((640, 128), F32),
        in_specs=[whole(pltpu.VMEM)] * 2,
        out_specs=whole(pltpu.VMEM),
        scratch_shapes=[pltpu.VMEM((2, 192, 256), BF16)],
        compiler_params=pltpu.CompilerParams(vmem_limit_bytes=16 * 2**20),
        name="volume_start",
    )(own, w1)


def volume_kernel(
    pos_ref, own_ref, next_ref, near_ref, part_ref, w1_ref, w2_ref, out_ref, x1, x2, acc, packed
):
    p = pos_ref[0]
    q = pos_ref[1]
    even = (1 - p % 2).astype(F32)
    odd = 1.0 - even
    for i in range(2):
        near = near_ref[i].astype(F32)
        nxt = next_ref[i].astype(F32)
        put_depth(x1, i, even * nxt + odd * near)
        put_depth(x1, 2 + i, even * near + odd * nxt)
    sums = [part_ref[i * 160 : (i + 1) * 160] for i in range(4)]
    for dy in range(3):
        rows = slice(dy * 16, dy * 16 + 160)
        low0 = dot_nt(x1[0:2, rows, :].reshape(320, 256), w1_ref[dy])
        low1 = dot_nt(x1[1, rows, :], w1_ref[3 + dy])
        high1 = dot_nt(x1[2, rows, :], w1_ref[3 + dy])
        high2 = dot_nt(x1[2:4, rows, :].reshape(320, 256), w1_ref[6 + dy])
        sums[0] = sums[0] + low0[0:160] + low1
        sums[1] = sums[1] + low0[160:320]
        sums[2] = sums[2] + high2[0:160]
        sums[3] = sums[3] + high2[160:320] + high1
    y = lax.broadcasted_iota(jnp.int32, (160, 128), 0) // 16
    first_y = jnp.where(q == 0, 1, 0)
    last_y = jnp.where(q == 3, 8, 9)
    inside = (y >= first_y) & (y <= last_y)
    for i in range(4):
        h = jnp.where(inside, jnp.maximum(sums[i], 0.0), 0.0)
        if i == 0:
            h = h * jnp.where(p == 0, 0.0, 1.0)
        if i == 3:
            h = h * jnp.where(p == 31, 0.0, 1.0)
        put_depth(x2, i, h)
    for t in range(9):
        dx, dy = divmod(t, 3)
        part = dot_nt(x2[dx : dx + 2, dy * 16 : dy * 16 + 128, :].reshape(256, 256), w2_ref[t])
        if t == 0:
            acc[...] = part
        else:
            acc[...] += part
    for i in range(2):
        res = acc[i * 128 : (i + 1) * 128] + own_ref[i, 32:160].astype(F32)
        res = res.T
        for k in range(4):
            block = [res[32 * z : 32 * z + 32, 32 * k : 32 * k + 32] for z in range(4)]
            packed[pl.ds(2 * k + i, 32, stride=8), :] = jnp.concatenate(block, axis=1)
    source = lax.broadcasted_iota(jnp.int32, (128, 128), 0)
    target = lax.broadcasted_iota(jnp.int32, (128, 128), 1)
    place = jnp.where(target == (source % 32) * 4 + source // 32, 1.0, 0.0).astype(BF16)
    out_ref[...] = dot(packed[...].astype(BF16), place).astype(BF16)


def volume_convs(pos, own, nxt, near, part, w1, w2):
    return pl.pallas_call(
        volume_kernel,
        out_shape=jax.ShapeDtypeStruct((256, 128), BF16),
        in_specs=[whole(pltpu.SMEM)] + [whole(pltpu.VMEM)] * 6,
        out_specs=whole(pltpu.VMEM),
        scratch_shapes=[
            pltpu.VMEM((4, 192, 256), BF16),
            pltpu.VMEM((4, 160, 256), BF16),
            pltpu.VMEM((256, 128), F32),
            pltpu.VMEM((256, 128), F32),
        ],
        compiler_params=pltpu.CompilerParams(vmem_limit_bytes=32 * 2**20),
        name="volume",
    )(pos, own, nxt, near, part, w1, w2)


def banded(weight):
    taps = weight.reshape(9, 3, 32, 32)
    zero = jnp.zeros((9, 32, 32), weight.dtype)
    rows = []
    for z in range(4):
        blocks = [zero] * 8
        for dz in range(3):
            at = z + dz - 1
            blocks[4 if at < 0 else 5 if at > 3 else at] = taps[:, dz]
        rows.append(jnp.concatenate(blocks, axis=2))
    return jnp.concatenate(rows, axis=1)


def swap(x, partner, cams, slabs):
    pairs = []
    for p in range(cams):
        for s in range(slabs):
            to = partner(p, s)
            if 0 <= to[0] < cams and 0 <= to[1] < slabs:
                pairs.append((p * slabs + s, to[0] * slabs + to[1]))
    return lax.ppermute(x, AXES, pairs)


def core_partner(p, s):
    return p, s ^ 1


def far_partner(p, s):
    return p, (s + 1 if s % 2 else s - 1)


def near_partner(p, s):
    return p ^ 1, s


def next_partner(p, s):
    return (p + 1 if p % 2 else p - 1), s


def local(
    image,
    w_first,
    w_second,
    w_reduce,
    cam_weight,
    sample_pixel,
    sample_frac,
    voxel_slot,
    wv_first,
    wv_second,
):
    cams = lax.axis_size("cam")
    slabs = lax.axis_size("slab")
    p = lax.axis_index("cam")
    s = lax.axis_index("slab")
    even = s % 2 == 0
    img = image[0]
    top, bottom = img[0:3], img[1:4]
    facing_far = jnp.where(even, top, bottom)
    far = swap(facing_far, far_partner, cams, slabs)
    later, _ = lax.optimization_barrier((img, facing_far))
    facing_core = jnp.where(even, later[1:4], later[0:3])
    core = swap(facing_core, core_partner, cams, slabs)

    pix = sample_pixel[0].T
    frac = jnp.transpose(sample_frac[0], (0, 2, 1))
    w1 = w_first.reshape(3, 384, 128)
    w2 = w_second.reshape(3, 384, 128)
    by_row = voxel_slot[0].reshape(1024, 4)
    by_lane = by_row.T
    band1 = banded(wv_first)
    band2 = banded(wv_second)
    slab_pos = s.astype(jnp.int32).reshape(1)

    part, weights, blends = prepare(cam_weight, img, w1, pix, frac)
    inner, ready = middle(slab_pos, core, w1, w2, w_reduce.T, part)
    sent = features(
        slab_pos, far, core, w1, w2, w_reduce.T, part, weights, blends, inner, ready
    )
    got = lax.all_to_all(sent.reshape(128, 8, 128), AXES, 0, 0, tiled=True).reshape(1024, 128)
    facing = facing_rows(got, slots(slab_pos, by_lane))
    facing, got = lax.optimization_barrier((facing, got))
    far = swap(facing, far_partner, cams, slabs)
    volume = scatter(got, by_lane, by_row)

    pos = jnp.stack([p, s]).astype(jnp.int32)
    top, bottom = volume[:, 0:32], volume[:, 96:128]
    core = swap(jnp.where(even, bottom, top), core_partner, cams, slabs)
    above = jnp.where(even, far, core)
    below = jnp.where(even, core, far)
    own = jnp.concatenate([above, volume, below], axis=1)
    nxt = swap(own, next_partner, cams, slabs)
    near = swap(own, near_partner, cams, slabs)
    part = volume_start(own, band1)
    out = volume_convs(pos, own, nxt, near, part, band1, band2)
    return out.reshape(32, 4, 2, 128).transpose(0, 2, 1, 3).reshape(32, 2, 512)


def solution(mesh):
    placed = (
        P(("dp", "cam"), "slab", None, None),
        P(),
        P(),
        P(),
        P("cam"),
        P(("dp", "cam", "slab"), None, None),
        P(("dp", "cam", "slab"), None, None, None),
        P(("dp", "cam", "slab"), None, None),
        P(),
        P(),
    )
    return jax.shard_map(
        local, mesh=mesh, in_specs=placed, out_specs=P(None, ("dp", "cam"), "slab"), check_vma=False
    )
```

```python
import jax
import jax.numpy as jnp
from jax import lax
from jax.experimental import pallas as pl
from jax.experimental.pallas import tpu as pltpu
from jax.sharding import PartitionSpec as P

AXES = ("cam", "slab")
F32 = jnp.float32
BF16 = jnp.bfloat16


def dot(a, b):
    return jnp.dot(a, b, preferred_element_type=F32)


def dot_nt(a, b):
    return lax.dot_general(a, b, (((1,), (1,)), ((), ())), preferred_element_type=F32)


def whole(memory_space):
    return pl.BlockSpec(memory_space=memory_space)


def put_columns(dst, row, x):
    cols = x.shape[0]
    pos = lax.broadcasted_iota(jnp.int32, x.shape, 0)
    left = jnp.where(pos == 0, 0.0, pltpu.roll(x, 1, 0))
    right = jnp.where(pos == cols - 1, 0.0, pltpu.roll(x, cols - 1, 0))
    dst[row, :, 0:128] = left.astype(BF16)
    dst[row, :, 128:256] = x.astype(BF16)
    dst[row, :, 256:384] = right.astype(BF16)


def lanes(x):
    return jnp.concatenate([x[i : i + 1] for i in range(4)], axis=1)


def sample_weights(scale_ref, pix_ref, frac_ref, weights, blends):
    scale = scale_ref[0]
    col_iota = lax.broadcasted_iota(jnp.int32, (256, 512), 0)
    row_iota = lax.broadcasted_iota(jnp.int32, (8, 512), 0)
    for k in range(8):
        pix = lanes(pix_ref[4 * k : 4 * k + 4])
        fr = lanes(frac_ref[0, 4 * k : 4 * k + 4])
        fc = lanes(frac_ref[1, 4 * k : 4 * k + 4])
        col = pix & 255
        row = pix >> 8
        weights[k] = jnp.where(
            col_iota == col, 1.0 - fc, jnp.where(col_iota == col + 1, fc, 0.0)
        ).astype(BF16)
        blends[k] = scale * jnp.where(
            row_iota == row, 1.0 - fr, jnp.where(row_iota == row + 1, fr, 0.0)
        )


def prepare_kernel(
    scale_ref, img_hbm, w1_hbm, pix_hbm, frac_hbm, acc, weights, blends,
    x1, img_ref, w1_ref, pix_ref, frac_ref, sems,
):
    pairs = ((pix_hbm, pix_ref), (frac_hbm, frac_ref), (img_hbm, img_ref), (w1_hbm, w1_ref))
    copies = [pltpu.make_async_copy(src, dst, sems.at[i]) for i, (src, dst) in enumerate(pairs)]
    for copy in copies:
        copy.start()
    copies[0].wait()
    copies[1].wait()
    sample_weights(scale_ref, pix_ref, frac_ref, weights, blends)
    copies[2].wait()
    copies[3].wait()
    for i in range(4):
        put_columns(x1, i, img_ref[i].astype(F32))
    own = x1[...].reshape(1024, 384)
    acc[0:512] = jnp.zeros((512, 128), F32)
    acc[1536:1792] = jnp.zeros((256, 128), F32)
    acc[512:1536] = dot(own, w1_ref[0])
    acc[256:1280] += dot(own, w1_ref[1])
    acc[0:1024] += dot(own, w1_ref[2])


def prepare(scale, img, w1, pix, frac):
    return pl.pallas_call(
        prepare_kernel,
        out_shape=(
            jax.ShapeDtypeStruct((1792, 128), F32),
            jax.ShapeDtypeStruct((8, 256, 512), BF16),
            jax.ShapeDtypeStruct((8, 8, 512), F32),
        ),
        in_specs=[whole(pltpu.SMEM)] + [whole(pltpu.HBM)] * 4,
        out_specs=(whole(pltpu.VMEM),) * 3,
        scratch_shapes=[
            pltpu.VMEM((4, 256, 384), BF16),
            pltpu.VMEM((4, 256, 128), BF16),
            pltpu.VMEM((3, 384, 128), BF16),
            pltpu.VMEM((32, 128), jnp.int32),
            pltpu.VMEM((2, 32, 128), F32),
            pltpu.SemaphoreType.DMA((4,)),
        ],
        compiler_params=pltpu.CompilerParams(vmem_limit_bytes=24 * 2**20),
        cost_estimate=pl.CostEstimate(flops=10000000000, bytes_accessed=4 * 10**6, transcendentals=0),
        name="prepare",
    )(scale, *(pltpu.with_memory_space_constraint(x, pltpu.HBM) for x in (img, w1, pix, frac)))


def table_rows(acc, at, count, wr):
    rows = []
    for i in range(at, at + count):
        h = jnp.maximum(acc[i * 256 : (i + 1) * 256], 0.0)
        rows.append(dot_nt(wr, h.astype(BF16)))
    return rows


def blended(table, first, weights, blend):
    got = dot(table, weights)
    total = got[0:32] * blend[first : first + 1]
    for r in range(1, got.shape[0] // 32):
        total = total + got[32 * r : 32 * r + 32] * blend[first + r : first + r + 1]
    return total


def middle_kernel(
    pos_ref, core_ref, w1_ref, w2_ref, wr_ref, part_ref, weights, blends, inner, rest, x1, x2, acc
):
    @pl.when(pos_ref[0] % 2 == 0)
    def _():
        for i in range(3):
            put_columns(x1, i, core_ref[i].astype(F32))
        tail0 = dot(x1[0], w1_ref[0])
        tail1 = dot(x1[0:2].reshape(512, 384), w1_ref[1])
        tail2 = dot(x1[0:3].reshape(768, 384), w1_ref[2])
        for i in range(2, 7):
            h = part_ref[i * 256 : (i + 1) * 256]
            if i == 4:
                h = h + tail2[0:256]
            elif i == 5:
                h = h + tail2[256:512] + tail1[0:256]
            elif i == 6:
                h = h + tail2[512:768] + tail1[256:512] + tail0
            put_columns(x2, i - 2, jnp.maximum(h, 0.0))
        inner[...] = x2[0:2]
        acc[...] = dot(x2[0:3].reshape(768, 384), w2_ref[0])
        acc[...] += dot(x2[1:4].reshape(768, 384), w2_ref[1])
        acc[...] += dot(x2[2:5].reshape(768, 384), w2_ref[2])
        table = jnp.concatenate(table_rows(acc, 0, 3, wr_ref[...]), axis=0).astype(BF16)
        for k in range(8):
            rest[k] = blended(table, 2, weights[k], blends[k])


def middle(slab, core, w1, w2, wr, part, weights, blends):
    return pl.pallas_call(
        middle_kernel,
        out_shape=(
            jax.ShapeDtypeStruct((2, 256, 384), BF16),
            jax.ShapeDtypeStruct((8, 32, 512), F32),
        ),
        in_specs=[whole(pltpu.SMEM)] + [whole(pltpu.VMEM)] * 7,
        out_specs=(whole(pltpu.VMEM),) * 2,
        scratch_shapes=[
            pltpu.VMEM((3, 256, 384), BF16),
            pltpu.VMEM((5, 256, 384), BF16),
            pltpu.VMEM((768, 128), F32),
        ],
        compiler_params=pltpu.CompilerParams(vmem_limit_bytes=24 * 2**20),
        cost_estimate=pl.CostEstimate(flops=1000000, bytes_accessed=10**3, transcendentals=0),
        name="middle",
    )(slab, core, w1, w2, wr, part, weights, blends)


def features_kernel(
    pos_ref, far_ref, core_ref, w1_ref, w2_ref, wr_ref, part_ref, weights, blends,
    inner, rest, out_ref, x1, x2, acc, packed,
):
    slab = pos_ref[0]
    not_first = jnp.where(slab == 0, 0.0, 1.0)
    not_last = jnp.where(slab == 3, 0.0, 1.0)

    def first_rows(above):
        for i in range(2):
            put_columns(x1, i, above[1 + i].astype(F32))
        head = dot(x1[0:2].reshape(512, 384), w1_ref[0])
        return head[0:256] + dot(x1[1], w1_ref[1]), head[256:512]

    def pack(k, total):
        block = jnp.concatenate([total[:, 128 * i : 128 * i + 128] for i in range(4)], axis=0)
        packed[pl.ds(k, 128, stride=8), :] = block.T

    @pl.when(slab % 2 == 0)
    def _():
        head0, head1 = first_rows(far_ref)
        put_columns(x2, 0, jnp.maximum(part_ref[0:256] + head0, 0.0) * not_first)
        put_columns(x2, 1, jnp.maximum(part_ref[256:512] + head1, 0.0))
        x2[2:4] = inner[...]
        acc[0:512] = dot(x2[0:2].reshape(512, 384), w2_ref[0])
        acc[0:512] += dot(x2[1:3].reshape(512, 384), w2_ref[1])
        acc[0:512] += dot(x2[2:4].reshape(512, 384), w2_ref[2])
        table = jnp.concatenate(table_rows(acc, 0, 2, wr_ref[...]), axis=0).astype(BF16)
        for k in range(8):
            pack(k, blended(table, 0, weights[k], blends[k]) + rest[k])

    @pl.when(slab % 2 == 1)
    def _():
        head0, head1 = first_rows(core_ref)
        for i in range(3):
            put_columns(x1, 2 + i, far_ref[i].astype(F32))
        tail0 = dot(x1[2], w1_ref[0])
        tail1 = dot(x1[2:4].reshape(512, 384), w1_ref[1])
        tail2 = dot(x1[2:5].reshape(768, 384), w1_ref[2])
        for i in range(7):
            h = part_ref[i * 256 : (i + 1) * 256]
            if i == 0:
                h = h + head0
            elif i == 1:
                h = h + head1
            elif i == 4:
                h = h + tail2[0:256]
            elif i == 5:
                h = h + tail2[256:512] + tail1[0:256]
            elif i == 6:
                h = h + tail2[512:768] + tail1[256:512] + tail0
            h = jnp.maximum(h, 0.0)
            if i >= 5:
                h = h * not_last
            put_columns(x2, i, h)
        acc[...] = dot(x2[0:5].reshape(1280, 384), w2_ref[0])
        acc[...] += dot(x2[1:6].reshape(1280, 384), w2_ref[1])
        acc[...] += dot(x2[2:7].reshape(1280, 384), w2_ref[2])
        rows = table_rows(acc, 0, 5, wr_ref[...])
        rows[4] = rows[4] * not_last
        table = jnp.concatenate(rows, axis=0).astype(BF16)
        for k in range(8):
            pack(k, blended(table, 0, weights[k], blends[k]))

    out_ref[...] = packed[...].astype(BF16)


def features(slab, far, core, w1, w2, wr, part, weights, blends, inner, rest):
    return pl.pallas_call(
        features_kernel,
        out_shape=jax.ShapeDtypeStruct((1024, 128), BF16),
        in_specs=[whole(pltpu.SMEM)] + [whole(pltpu.VMEM)] * 10,
        out_specs=whole(pltpu.VMEM),
        scratch_shapes=[
            pltpu.VMEM((5, 256, 384), BF16),
            pltpu.VMEM((7, 256, 384), BF16),
            pltpu.VMEM((1280, 128), F32),
            pltpu.VMEM((1024, 128), F32),
        ],
        compiler_params=pltpu.CompilerParams(vmem_limit_bytes=32 * 2**20),
        name="features",
    )(slab, far, core, w1, w2, wr, part, weights, blends, inner, rest)


def slots_kernel(pos_ref, by_lane_ref, one_hot):
    row = lax.broadcasted_iota(jnp.int32, (256, 1024), 0)
    start = (pos_ref[0] % 2) * 96
    voxel = (row // 32 % 2 * 128 + start + row % 32) * 4 + row // 64
    for s in range(4):
        hit = voxel == by_lane_ref[s : s + 1]
        one_hot[:, 1024 * s : 1024 * s + 1024] = jnp.where(hit, 1.0, 0.0).astype(BF16)


def slots(slab, by_lane):
    return pl.pallas_call(
        slots_kernel,
        out_shape=jax.ShapeDtypeStruct((256, 4096), BF16),
        in_specs=[whole(pltpu.SMEM), whole(pltpu.VMEM)],
        out_specs=whole(pltpu.VMEM),
        compiler_params=pltpu.CompilerParams(vmem_limit_bytes=16 * 2**20),
        cost_estimate=pl.CostEstimate(flops=10**7, bytes_accessed=2 * 10**6, transcendentals=0),
        name="slots",
    )(slab, by_lane)


def facing_kernel(val_ref, one_hot, out_ref):
    group = lax.broadcasted_iota(jnp.int32, (256, 128), 1) // 32
    val = val_ref[...]
    total = jnp.zeros((256, 128), F32)
    for s in range(4):
        part = dot(one_hot[:, 1024 * s : 1024 * s + 1024], val)
        total = jnp.where(group == s, part, total)
    total = total + pltpu.roll(total, 64, 1)
    total = total + pltpu.roll(total, 32, 1)
    group = group[0:64]
    rows = jnp.zeros((64, 128), F32)
    for z in range(4):
        rows = jnp.where(group == z, total[64 * z : 64 * z + 64], rows)
    out_ref[...] = rows.reshape(2, 32, 128).astype(BF16)


def facing_rows(val, one_hot):
    return pl.pallas_call(
        facing_kernel,
        out_shape=jax.ShapeDtypeStruct((2, 32, 128), BF16),
        in_specs=[whole(pltpu.VMEM)] * 2,
        out_specs=whole(pltpu.VMEM),
        compiler_params=pltpu.CompilerParams(vmem_limit_bytes=16 * 2**20),
        name="facing",
    )(val, one_hot)


def scatter_kernel(val_ref, by_lane_ref, by_row_ref, out_ref):
    val = val_ref[...]
    lo_iota = lax.broadcasted_iota(jnp.int32, (256, 1024), 0)
    hi_iota = lax.broadcasted_iota(jnp.int32, (1024, 128), 1) // 32
    sel_row = lax.broadcasted_iota(jnp.int32, (128, 128), 0)
    sel_col = lax.broadcasted_iota(jnp.int32, (128, 128), 1) % 32
    total = jnp.zeros((256, 128), F32)
    for s in range(4):
        one_hot = jnp.where(lo_iota == (by_lane_ref[s : s + 1] >> 2), 1.0, 0.0).astype(BF16)
        select = jnp.where(sel_row == sel_col + 32 * s, 1.0, 0.0).astype(BF16)
        spread = dot(val, select)
        hi = by_row_ref[:, s : s + 1] & 3
        spread = jnp.where(hi_iota == hi, spread, 0.0).astype(BF16)
        total = total + dot(one_hot, spread)
    out_ref[...] = total.reshape(2, 128, 128).astype(BF16)


def scatter(val, by_lane, by_row):
    return pl.pallas_call(
        scatter_kernel,
        out_shape=jax.ShapeDtypeStruct((2, 128, 128), BF16),
        in_specs=[whole(pltpu.VMEM)] * 3,
        out_specs=whole(pltpu.VMEM),
        compiler_params=pltpu.CompilerParams(vmem_limit_bytes=16 * 2**20),
        cost_estimate=pl.CostEstimate(flops=3 * 10**8, bytes_accessed=3 * 10**6, transcendentals=0),
        name="scatter",
    )(val, by_lane, by_row)


def put_depth(dst, plane, x):
    step = lax.broadcasted_iota(jnp.int32, x.shape, 0) % 16
    lane = lax.broadcasted_iota(jnp.int32, x.shape, 1)
    rows = x.shape[0]
    before = jnp.where(step == 0, 0.0, pltpu.roll(x, 1, 0))
    after = jnp.where(step == 15, 0.0, pltpu.roll(x, rows - 1, 0))
    side = pltpu.roll(jnp.where(lane >= 96, before, after), 32, 1)
    dst[plane, :, 0:128] = x.astype(BF16)
    dst[plane, :, 128:256] = jnp.where(lane < 64, side, 0.0).astype(BF16)


def volume_start_kernel(own_ref, w_ref, acc, x1):
    for i in range(2):
        put_depth(x1, i, own_ref[i].astype(F32))
    zero = jnp.zeros((160, 128), F32)
    acc[0:160] = zero
    acc[480:640] = zero
    for k, dx in enumerate((1, 0, 2)):
        total = None
        for dy in range(3):
            rows = x1[:, dy * 16 : dy * 16 + 160, :].reshape(320, 256)
            part = dot_nt(rows, w_ref[dx * 3 + dy])
            total = part if total is None else total + part
        at = (2 - dx) * 160
        if k == 0:
            acc[at : at + 320] = total
        else:
            acc[at : at + 320] += total


def volume_start(own, w1):
    return pl.pallas_call(
        volume_start_kernel,
        out_shape=jax.ShapeDtypeStruct((640, 128), F32),
        in_specs=[whole(pltpu.VMEM)] * 2,
        out_specs=whole(pltpu.VMEM),
        scratch_shapes=[pltpu.VMEM((2, 192, 256), BF16)],
        compiler_params=pltpu.CompilerParams(vmem_limit_bytes=16 * 2**20),
        name="volume_start",
    )(own, w1)


def volume_kernel(
    pos_ref, own_ref, next_ref, near_ref, part_ref, w1_ref, w2_ref, out_ref, x1, x2, acc, packed
):
    p = pos_ref[0]
    q = pos_ref[1]
    even = (1 - p % 2).astype(F32)
    odd = 1.0 - even
    for i in range(2):
        near = near_ref[i].astype(F32)
        nxt = next_ref[i].astype(F32)
        put_depth(x1, i, even * nxt + odd * near)
        put_depth(x1, 2 + i, even * near + odd * nxt)
    sums = [part_ref[i * 160 : (i + 1) * 160] for i in range(4)]
    for dy in range(3):
        rows = slice(dy * 16, dy * 16 + 160)
        low0 = dot_nt(x1[0:2, rows, :].reshape(320, 256), w1_ref[dy])
        low1 = dot_nt(x1[1, rows, :], w1_ref[3 + dy])
        high1 = dot_nt(x1[2, rows, :], w1_ref[3 + dy])
        high2 = dot_nt(x1[2:4, rows, :].reshape(320, 256), w1_ref[6 + dy])
        sums[0] = sums[0] + low0[0:160] + low1
        sums[1] = sums[1] + low0[160:320]
        sums[2] = sums[2] + high2[0:160]
        sums[3] = sums[3] + high2[160:320] + high1
    y = lax.broadcasted_iota(jnp.int32, (160, 128), 0) // 16
    first_y = jnp.where(q == 0, 1, 0)
    last_y = jnp.where(q == 3, 8, 9)
    inside = (y >= first_y) & (y <= last_y)
    for i in range(4):
        h = jnp.where(inside, jnp.maximum(sums[i], 0.0), 0.0)
        if i == 0:
            h = h * jnp.where(p == 0, 0.0, 1.0)
        if i == 3:
            h = h * jnp.where(p == 31, 0.0, 1.0)
        put_depth(x2, i, h)
    for t in range(9):
        dx, dy = divmod(t, 3)
        part = dot_nt(x2[dx : dx + 2, dy * 16 : dy * 16 + 128, :].reshape(256, 256), w2_ref[t])
        if t == 0:
            acc[...] = part
        else:
            acc[...] += part
    for i in range(2):
        res = acc[i * 128 : (i + 1) * 128] + own_ref[i, 32:160].astype(F32)
        res = res.T
        for k in range(4):
            block = [res[32 * z : 32 * z + 32, 32 * k : 32 * k + 32] for z in range(4)]
            packed[pl.ds(2 * k + i, 32, stride=8), :] = jnp.concatenate(block, axis=1)
    source = lax.broadcasted_iota(jnp.int32, (128, 128), 0)
    target = lax.broadcasted_iota(jnp.int32, (128, 128), 1)
    place = jnp.where(target == (source % 32) * 4 + source // 32, 1.0, 0.0).astype(BF16)
    out_ref[...] = dot(packed[...].astype(BF16), place).astype(BF16)


def volume_convs(pos, own, nxt, near, part, w1, w2):
    return pl.pallas_call(
        volume_kernel,
        out_shape=jax.ShapeDtypeStruct((256, 128), BF16),
        in_specs=[whole(pltpu.SMEM)] + [whole(pltpu.VMEM)] * 6,
        out_specs=whole(pltpu.VMEM),
        scratch_shapes=[
            pltpu.VMEM((4, 192, 256), BF16),
            pltpu.VMEM((4, 160, 256), BF16),
            pltpu.VMEM((256, 128), F32),
            pltpu.VMEM((256, 128), F32),
        ],
        compiler_params=pltpu.CompilerParams(vmem_limit_bytes=32 * 2**20),
        name="volume",
    )(pos, own, nxt, near, part, w1, w2)


def banded(weight):
    taps = weight.reshape(9, 3, 32, 32)
    zero = jnp.zeros((9, 32, 32), weight.dtype)
    rows = []
    for z in range(4):
        blocks = [zero] * 8
        for dz in range(3):
            at = z + dz - 1
            blocks[4 if at < 0 else 5 if at > 3 else at] = taps[:, dz]
        rows.append(jnp.concatenate(blocks, axis=2))
    return jnp.concatenate(rows, axis=1)


def swap(x, partner, cams, slabs):
    pairs = []
    for p in range(cams):
        for s in range(slabs):
            to = partner(p, s)
            if 0 <= to[0] < cams and 0 <= to[1] < slabs:
                pairs.append((p * slabs + s, to[0] * slabs + to[1]))
    return lax.ppermute(x, AXES, pairs)


def core_partner(p, s):
    return p, s ^ 1


def far_partner(p, s):
    return p, (s + 1 if s % 2 else s - 1)


def near_partner(p, s):
    return p ^ 1, s


def next_partner(p, s):
    return (p + 1 if p % 2 else p - 1), s


def local(
    image,
    w_first,
    w_second,
    w_reduce,
    cam_weight,
    sample_pixel,
    sample_frac,
    voxel_slot,
    wv_first,
    wv_second,
):
    cams = lax.axis_size("cam")
    slabs = lax.axis_size("slab")
    p = lax.axis_index("cam")
    s = lax.axis_index("slab")
    even = s % 2 == 0
    img = image[0]
    top, bottom = img[0:3], img[1:4]
    far = swap(jnp.where(even, top, bottom), far_partner, cams, slabs)
    core = swap(jnp.where(even, bottom, top), core_partner, cams, slabs)

    pix = sample_pixel[0].T
    frac = jnp.transpose(sample_frac[0], (0, 2, 1))
    w1 = w_first.reshape(3, 384, 128)
    w2 = w_second.reshape(3, 384, 128)
    by_row = voxel_slot[0].reshape(1024, 4)
    by_lane = by_row.T
    band1 = banded(wv_first)
    band2 = banded(wv_second)
    slab_pos = s.astype(jnp.int32).reshape(1)

    part, weights, blends = prepare(cam_weight, img, w1, pix, frac)
    inner, rest = middle(slab_pos, core, w1, w2, w_reduce.T, part, weights, blends)
    sent = features(
        slab_pos, far, core, w1, w2, w_reduce.T, part, weights, blends, inner, rest
    )
    got = lax.all_to_all(sent.reshape(128, 8, 128), AXES, 0, 0, tiled=True).reshape(1024, 128)
    facing = facing_rows(got, slots(slab_pos, by_lane))
    facing, got = lax.optimization_barrier((facing, got))
    far = swap(facing, far_partner, cams, slabs)
    volume = scatter(got, by_lane, by_row)

    pos = jnp.stack([p, s]).astype(jnp.int32)
    top, bottom = volume[:, 0:32], volume[:, 96:128]
    core = swap(jnp.where(even, bottom, top), core_partner, cams, slabs)
    above = jnp.where(even, far, core)
    below = jnp.where(even, core, far)
    own = jnp.concatenate([above, volume, below], axis=1)
    nxt = swap(own, next_partner, cams, slabs)
    near = swap(own, near_partner, cams, slabs)
    part = volume_start(own, band1)
    out = volume_convs(pos, own, nxt, near, part, band1, band2)
    return out.reshape(32, 4, 2, 128).transpose(0, 2, 1, 3).reshape(32, 2, 512)


def solution(mesh):
    placed = (
        P(("dp", "cam"), "slab", None, None),
        P(),
        P(),
        P(),
        P("cam"),
        P(("dp", "cam", "slab"), None, None),
        P(("dp", "cam", "slab"), None, None, None),
        P(("dp", "cam", "slab"), None, None),
        P(),
        P(),
    )
    return jax.shard_map(
        local, mesh=mesh, in_specs=placed, out_specs=P(None, ("dp", "cam"), "slab"), check_vma=False
    )
```
